128 devices in a mesh: ctx: 16 (over x, y), head: 8 (over z, core).
Axes of the slice: x: 4, y: 4, z: 4, core: 2. Of those that a mesh axis runs over, the one named last changes fastest.
Arguments:
- tokens: bfloat16 [8192, 5376], P('ctx'), may hold values from -16 to 16
- norm_gain: bfloat16 [5376], replicated, may hold values from 0.099609375 to 1.8984375
- w_query: bfloat16 [5376, 4096], P(None, 'head'), may hold values from -4 to 4
- w_key: bfloat16 [5376, 2048], P(None, 'head'), may hold values from -1 to 1
- value_weight: bfloat16 [5376, 2048], P(None, 'head'), may hold values from -0.078125 to 0.078125
- w_out: bfloat16 [4096, 5376], P('head'), may hold values from -0.09375 to 0.09375
- mask_logit: float32 [32], P('head'), may hold values from -2 to 2
- noise_draw: float32 [32], P('head'), may hold values from 0.02 to 0.98
- cotangent: bfloat16 [8192, 5376], P('ctx'), may hold values from -16 to 16
Outputs:
- layer_out: bfloat16 [8192, 5376], P('ctx', 'head')
- grad_logit: float32 [32], P('head')
- grad_out_proj: float32 [4096, 5376], P('head', 'ctx')
The draws below stay inside these ranges and needn't reach their ends.
All inputs are finite; a program needn't handle non-finite values.
Results may differ from the reference program's by a relative error of at most 0.025.
Values may be sent and summed in bfloat16 or wider, within the bound.
A program may use at most 128 MiB of HBM per device.

```python
import math
import jax
import jax.numpy as jnp
from jax import lax

MODEL_WIDTH = 5376
QUERY_HEADS = 32
KEY_VALUE_HEADS = 16
HEAD_SIZE = 128
WINDOW_TOKENS = 1024
TOKENS = 8192
N_HEAD = 8


def draw_tokens(key, part):
    normal_rows = jax.random.normal(jax.random.fold_in(key, 11), (TOKENS, MODEL_WIDTH), jnp.float32)
    values = normal_rows
    return jnp.clip(values, -16.0, 16.0).astype(jnp.bfloat16)


def projection_pair(key):
    key_portion = jax.random.normal(jax.random.fold_in(key, 21), (MODEL_WIDTH, KEY_VALUE_HEADS * HEAD_SIZE), jnp.float32) / math.sqrt(MODEL_WIDTH)
    extra = jax.random.normal(jax.random.fold_in(key, 22), (MODEL_WIDTH, QUERY_HEADS * HEAD_SIZE), jnp.float32) / math.sqrt(MODEL_WIDTH)
    query_part = 2.3 * extra
    return (jnp.clip(query_part, -4.0, 4.0), jnp.clip(key_portion, -1.0, 1.0))


def draw_w_query(key, part):
    return projection_pair(key)[0].astype(jnp.bfloat16)


def draw_w_key(key, part):
    return projection_pair(key)[1].astype(jnp.bfloat16)


def draw_cotangent(key, part):
    position = jnp.arange(TOKENS, dtype=jnp.float32) / max(TOKENS - 1, 1)
    rising = (3.0 ** position)[:, None]
    values = rising * jax.random.normal(jax.random.fold_in(key, 33), (TOKENS, MODEL_WIDTH), jnp.float32)
    return jnp.clip(values, -16.0, 16.0).astype(jnp.bfloat16)


def steps_of(key, dims, cuts, low, high):
    def one(dim, shards_of):
        heights = jax.random.uniform(jax.random.fold_in(jax.random.fold_in(key, 6), dim), (shards_of,), jnp.float32, low / len(cuts), high / len(cuts))
        return jnp.repeat(jnp.exp(heights), dims[dim] // shards_of).reshape((-1,) + (1,) * (len(dims) - dim - 1))

    factor_of = one(*cuts[0])
    for cut in cuts[1:]:
        factor_of = factor_of * one(*cut)
    return factor_of


def bell_draw(own_key, extent, scale, reach, pieces=(), kind=jnp.bfloat16):
    entries = scale * jax.random.normal(own_key, extent, jnp.float32)
    if pieces:
        entries = entries * steps_of(own_key, extent, pieces, -0.22, 0.18)
    return jnp.clip(entries, -reach, reach).astype(kind)


def setup_inputs(seed: int = 0) -> dict:
    key_of = jax.random.split(jax.random.key(seed), 10)
    tokens = draw_tokens(jax.random.fold_in(key_of[9], 71), 0)
    norm_gain = jnp.clip(1.0 + 0.18 * jax.random.normal(key_of[1], (MODEL_WIDTH,), jnp.float32), 0.099609375, 1.8984375).astype(jnp.bfloat16)
    w_query = draw_w_query(jax.random.fold_in(key_of[9], 71), 0)
    w_key = draw_w_key(jax.random.fold_in(key_of[9], 71), 0)
    value_weight = bell_draw(key_of[4], (MODEL_WIDTH, KEY_VALUE_HEADS * HEAD_SIZE), MODEL_WIDTH ** -0.5, 0.078125, ((1, 8),))
    w_out = bell_draw(key_of[5], (QUERY_HEADS * HEAD_SIZE, MODEL_WIDTH), (QUERY_HEADS * HEAD_SIZE) ** -0.5, 0.09375, ((0, 8),))
    mask_logit = jnp.clip(jax.random.uniform(key_of[6], (QUERY_HEADS,), jnp.float32, -2.0, 2.0) * steps_of(key_of[6], (QUERY_HEADS,), ((0, 8),), -0.4, 0.0), -2.0, 2.0)
    noise_draw = jnp.clip(0.02 + 0.96000002 * jax.random.uniform(key_of[7], (QUERY_HEADS,), jnp.float32) ** steps_of(key_of[7], (QUERY_HEADS,), ((0, 8),), -0.2, 0.2), 0.02, 0.98)
    cotangent = draw_cotangent(jax.random.fold_in(key_of[9], 71), 0)
    return dict(tokens=tokens, norm_gain=norm_gain, w_query=w_query, w_key=w_key, value_weight=value_weight, w_out=w_out, mask_logit=mask_logit, noise_draw=noise_draw, cotangent=cotangent)


EPSILON = 1e-06
BETA = 2.0 / 3.0
GAMMA = -0.1
ZETA = 1.1
PENALTY = 0.1
SCORE_SCALE = 168.0 ** (-0.5)
TRANSPOSED = (((0,), (0,)), ((), ()))

def hard_concrete(mask_logit, noise_draw):
    logit = mask_logit.astype(jnp.float32)
    uniform_value = noise_draw.astype(jnp.float32)
    stretched = jax.nn.sigmoid((jnp.log(uniform_value) - jnp.log(1.0 - uniform_value) + logit) / BETA)
    shifted = stretched * (ZETA - GAMMA) + GAMMA
    gate_value = jnp.clip(shifted, 0.0, 1.0)
    inside = jnp.logical_and(shifted > 0.0, shifted < 1.0)
    gate_slope = jnp.where(inside, (ZETA - GAMMA) * stretched * (1.0 - stretched) / BETA, 0.0)
    expected = jax.nn.sigmoid(logit - BETA * math.log(-GAMMA / ZETA))
    return (gate_value, gate_slope, PENALTY * expected * (1.0 - expected))

def attend(query_rows, rows_of_keys, rows_of_values):
    every_row = query_rows.shape[0]
    rows_per_block = math.gcd(every_row, 512)
    group_count_heads = QUERY_HEADS // KEY_VALUE_HEADS
    blocks_of_queries = query_rows.reshape(every_row // rows_per_block, rows_per_block, KEY_VALUE_HEADS, group_count_heads, HEAD_SIZE)
    pad_amount = jnp.zeros((WINDOW_TOKENS, KEY_VALUE_HEADS * HEAD_SIZE), rows_of_keys.dtype)
    padded_keys = jnp.concatenate([pad_amount, rows_of_keys], axis=0).reshape(WINDOW_TOKENS + every_row, KEY_VALUE_HEADS, HEAD_SIZE)
    padded_values = jnp.concatenate([pad_amount, rows_of_values], axis=0).reshape(WINDOW_TOKENS + every_row, KEY_VALUE_HEADS, HEAD_SIZE)

    def one_block(block_index):
        first_row = block_index * rows_per_block
        query_block = lax.dynamic_index_in_dim(blocks_of_queries, block_index, 0, keepdims=False)
        key_block = lax.dynamic_slice_in_dim(padded_keys, first_row, WINDOW_TOKENS + rows_per_block, 0)
        value_block = lax.dynamic_slice_in_dim(padded_values, first_row, WINDOW_TOKENS + rows_per_block, 0)
        scores = jnp.einsum('rkgd,lkd->kgrl', query_block.astype(jnp.float32), key_block.astype(jnp.float32)) * SCORE_SCALE
        query_pos = first_row + jnp.arange(rows_per_block, dtype=jnp.int32)[:, None]
        key_pos = first_row - WINDOW_TOKENS + jnp.arange(WINDOW_TOKENS + rows_per_block, dtype=jnp.int32)[None, :]
        allowed = (key_pos <= query_pos) & (query_pos - key_pos < WINDOW_TOKENS) & (key_pos >= 0)
        scores = jnp.where(allowed, scores, -jnp.inf)
        row_max = lax.optimization_barrier(jnp.max(scores, axis=-1, keepdims=True))
        lifted = jnp.exp(scores - row_max)
        prob_rows = (lifted / lax.optimization_barrier(jnp.sum(lifted, axis=-1, keepdims=True))).astype(jnp.bfloat16)
        attended = jnp.einsum('kgrl,lkd->rkgd', prob_rows.astype(jnp.float32), value_block.astype(jnp.float32))
        return attended.astype(jnp.bfloat16).reshape(rows_per_block, QUERY_HEADS * HEAD_SIZE)
    blocks = lax.map(one_block, jnp.arange(every_row // rows_per_block, dtype=jnp.int32))
    return blocks.reshape(every_row, QUERY_HEADS * HEAD_SIZE)

def reference(tokens, norm_gain, w_query, w_key, value_weight, w_out, mask_logit, noise_draw, cotangent):
    widened = tokens.astype(jnp.float32)
    moment = lax.optimization_barrier(jnp.mean(jnp.square(widened), axis=1, keepdims=True))
    normed = (widened * lax.rsqrt(moment + EPSILON) * norm_gain.astype(jnp.float32)[None, :]).astype(jnp.bfloat16)
    query_rows = jnp.dot(normed, w_query, preferred_element_type=jnp.float32).astype(jnp.bfloat16)
    rows_of_keys = jnp.dot(normed, w_key, preferred_element_type=jnp.float32).astype(jnp.bfloat16)
    rows_of_values = jnp.dot(normed, value_weight, preferred_element_type=jnp.float32).astype(jnp.bfloat16)
    attended = attend(query_rows, rows_of_keys, rows_of_values)
    gate_value, gate_slope, penalty_term = hard_concrete(mask_logit, noise_draw)
    gate_columns = jnp.repeat(gate_value, HEAD_SIZE)
    gated = (attended.astype(jnp.float32) * gate_columns[None, :]).astype(jnp.bfloat16)
    group_width = QUERY_HEADS * HEAD_SIZE // N_HEAD
    gated_groups = gated.reshape(TOKENS, N_HEAD, group_width)
    weight_groups = w_out.reshape(N_HEAD, group_width, MODEL_WIDTH)

    def add_group(running, group_index):
        piece_in = lax.dynamic_index_in_dim(gated_groups, group_index, 1, keepdims=False)
        piece_weight = lax.dynamic_index_in_dim(weight_groups, group_index, 0, keepdims=False)
        partial_out = jnp.dot(piece_in, piece_weight, preferred_element_type=jnp.float32).astype(jnp.bfloat16)
        partial_out = lax.optimization_barrier(partial_out)
        return (running + partial_out.astype(jnp.float32), None)
    summed_out, unused = lax.scan(add_group, jnp.zeros((TOKENS, MODEL_WIDTH), jnp.float32), jnp.arange(N_HEAD, dtype=jnp.int32))
    layer_out = summed_out.astype(jnp.bfloat16)
    inv_root = 1.0 / math.sqrt(TOKENS)
    through = lax.dot_general(cotangent, w_out, (((1,), (1,)), ((), ())), preferred_element_type=jnp.float32)
    gate_product = lax.optimization_barrier(jnp.sum((through * attended.astype(jnp.float32)).reshape(TOKENS, QUERY_HEADS, HEAD_SIZE), axis=(0, 2))) * inv_root
    grad_logit = gate_product * gate_slope + penalty_term
    weight_sum = lax.dot_general(attended, cotangent, TRANSPOSED, preferred_element_type=jnp.float32)
    grad_out_proj = weight_sum * gate_columns[:, None] * inv_root
    return (layer_out, grad_logit, grad_out_proj)
```

```python
import functools
import math

import jax
import jax.numpy as jnp
from jax import lax
from jax.experimental import pallas as pl
from jax.experimental.pallas import tpu as pltpu
from jax.sharding import PartitionSpec as P

HEAD_SIZE = 128
WINDOW_TOKENS = 1024


EPSILON = 1e-06
BETA = 2.0 / 3.0
GAMMA = -0.1
ZETA = 1.1
PENALTY = 0.1
SCORE_SCALE = 168.0 ** (-0.5)
TRANSPOSED = (((0,), (0,)), ((), ()))


MESH = pl.DeviceIdType.MESH
BF16 = jnp.bfloat16
F32 = jnp.float32
GRAD_ROWS = 336
OUT_ROWS = 672
HALF_OUT = 336
SPLIT = 176


class Links:
    def __init__(self, send, recv):
        self.send, self.recv, self.count, self.open = send, recv, 0, []

    def start(self, source, target, device):
        copy = pltpu.make_async_remote_copy(
            src_ref=source,
            dst_ref=target,
            send_sem=self.send.at[self.count],
            recv_sem=self.recv.at[self.count],
            device_id=device,
            device_id_type=MESH,
        )
        self.count += 1
        copy.start()
        self.open.append(copy)
        return copy

    def finish(self):
        for copy in self.open:
            copy.wait_send()


def wide(value):
    return value.astype(F32)


def reduce_kernel(
    att, gated, cot_t, wout_t, grad_out, layer_out, gate_out,
    grad, grad_in, line, line_in, out, out_core, out_in, gate_acc, gate_in, send, recv,
):
    ctx, head = lax.axis_index("ctx"), lax.axis_index("head")
    px, py = ctx // 4, ctx % 4
    pz, core = head // 2, head % 2

    def at_x(step):
        return ((px + step) % 4 * 4 + py, head)

    def at_y(step):
        return (px * 4 + (py + step) % 4, head)

    def at_z(step):
        return (ctx, (pz + step) % 4 * 2 + core)

    sibling = (ctx, pz * 2 + (1 - core))
    places = {"x": (px, at_x), "y": (py, at_y)}
    peers = [at(step) for at in (at_x, at_y) for step in (1, 2, 3)] + [at_z(1), at_z(3), sibling]
    barrier = pltpu.get_barrier_semaphore()
    for peer in peers:
        pl.semaphore_signal(barrier, inc=1, device_id=peer, device_id_type=MESH)
    pl.semaphore_wait(barrier, len(peers))
    links = Links(send, recv)

    def block_of(number, first, target, half):
        if first == "y":
            return grad.at[number, pl.ds(2 * half, 2), target]
        return grad.at[number, target, pl.ds(2 * half, 2)]

    firsts = ["y", "x", "y", "x"]
    gate_acc[...] = jnp.zeros_like(gate_acc)
    gate_in[0] = jnp.zeros((8, 128), F32)

    def grad_pair(pair):
        def chunk(index, carry):
            rows = pl.ds(pl.multiple_of(index * GRAD_ROWS, 16), GRAD_ROWS)
            product = jnp.dot(
                cot_t[rows, :], att[:, 256 * pair : 256 * pair + 256], preferred_element_type=F32
            )
            for side in range(2):
                number = 2 * pair + side
                mine = product[:, 128 * side : 128 * side + 128]
                grad[number, index // 4, index % 4] = mine.astype(BF16)
                weighed = mine * wide(wout_t[rows, 128 * number : 128 * number + 128])
                gate_acc[number] += jnp.sum(weighed.reshape(GRAD_ROWS // 8, 8, 128), axis=0)
            return carry

        lax.fori_loop(0, 16, chunk, 0)

    stage1 = {}

    def send_first(number):
        first = firsts[number]
        place, at = places[first]
        far, after, before = (place + 2) % 4, (place + 1) % 4, (place + 3) % 4
        box = grad_in.at[number]
        stage1[number] = [
            links.start(block_of(number, first, far, 0), box.at[0], at(1)),
            links.start(block_of(number, first, far, 1), box.at[1], at(3)),
            links.start(block_of(number, first, before, 0), box.at[2], at(3)),
            links.start(block_of(number, first, after, 1), box.at[3], at(1)),
        ]

    def relay_first(number):
        first = firsts[number]
        place, at = places[first]
        after, before = (place + 1) % 4, (place + 3) % 4
        box = grad_in.at[number]
        for slot, target, half, step in ((0, after, 0, 1), (1, before, 1, 3)):
            stage1[number][slot].wait_recv()
            box[slot] = (wide(box[slot]) + wide(block_of(number, first, target, half)[...])).astype(BF16)
            stage1[number].append(links.start(box.at[slot], box.at[4 + slot], at(step)))

    def end_first(number):
        first = firsts[number]
        place, _ = places[first]
        box = grad_in.at[number]
        for half in range(2):
            stage1[number][2 + half].wait_recv()
            stage1[number][4 + half].wait_recv()
            total = wide(block_of(number, first, place, half)[...]) + wide(box[2 + half]) + wide(box[4 + half])
            line[number, pl.ds(2 * half, 2)] = total.astype(BF16)

    stage2 = {}
    cuts = (pl.ds(0, SPLIT), pl.ds(SPLIT, GRAD_ROWS - SPLIT))
    sizes = (pl.ds(0, SPLIT), pl.ds(0, GRAD_ROWS - SPLIT))

    def send_second(number):
        place, at = places["x" if firsts[number] == "y" else "y"]
        far, after, before = (place + 2) % 4, (place + 1) % 4, (place + 3) % 4
        mine, box = line.at[number], line_in.at[number]
        stage2[number] = [
            links.start(mine.at[far, cuts[0]], box.at[0, sizes[0]], at(1)),
            links.start(mine.at[far, cuts[1]], box.at[1, sizes[1]], at(3)),
            links.start(mine.at[before, cuts[0]], box.at[2, sizes[0]], at(3)),
            links.start(mine.at[after, cuts[1]], box.at[3, sizes[1]], at(1)),
        ]

    def relay_second(number):
        place, at = places["x" if firsts[number] == "y" else "y"]
        after, before = (place + 1) % 4, (place + 3) % 4
        mine, box = line.at[number], line_in.at[number]
        for slot, target, step in ((0, after, 1), (1, before, 3)):
            stage2[number][slot].wait_recv()
            part = box.at[slot, sizes[slot]]
            part[...] = (wide(part[...]) + wide(mine[target, cuts[slot]])).astype(BF16)
            stage2[number].append(links.start(part, box.at[4 + slot, sizes[slot]], at(step)))

    def end_second(number):
        place, _ = places["x" if firsts[number] == "y" else "y"]
        mine, box = line.at[number], line_in.at[number]
        for half in range(2):
            stage2[number][2 + half].wait_recv()
            stage2[number][4 + half].wait_recv()
            grad_out[number, cuts[half]] = (
                wide(mine[place, cuts[half]])
                + wide(box[2 + half, sizes[half]])
                + wide(box[4 + half, sizes[half]])
            )

    def out_part(which, place):
        def piece(index, carry):
            row = pl.multiple_of(index * 112, 16)
            source = pl.multiple_of((place * 2 + which) * OUT_ROWS + index * 112, 16)
            product = lax.dot_general(
                wout_t[pl.ds(source, 112), :], gated[...], (((1,), (1,)), ((), ())),
                preferred_element_type=F32,
            )
            out[which, place, pl.ds(row, 112), :] = product.astype(BF16)
            return carry

        lax.fori_loop(0, OUT_ROWS // 112, piece, 0)

    grad_pair(0)
    send_first(0)
    send_first(1)
    order = [(pz + step) % 4 for step in (2, 1, 3, 0)]
    across = []
    for place in order[:2]:
        out_part(1 - core, place)
        across.append(links.start(out.at[1 - core, place], out_core.at[place], sibling))
    grad_pair(1)
    send_first(2)
    send_first(3)
    for place in order[2:]:
        out_part(1 - core, place)
        across.append(links.start(out.at[1 - core, place], out_core.at[place], sibling))

    for number in range(4):
        gate_in[0, pl.ds(number, 1)] = jnp.sum(gate_acc[number], axis=0, keepdims=True)
    gate_y = [links.start(gate_in.at[0], gate_in.at[step], at_y(step)) for step in (1, 2, 3)]
    relay_first(0)
    relay_first(1)
    for place in order:
        out_part(core, place)

    def add_core(index):
        across[index].wait_recv()
        place = order[index]

        def piece(step, carry):
            rows = pl.ds(pl.multiple_of(step * 112, 16), 112)
            out[core, place, rows] = (wide(out[core, place, rows]) + wide(out_core[place, rows])).astype(BF16)
            return carry

        lax.fori_loop(0, OUT_ROWS // 112, piece, 0)

    far, after, before = order[0], order[1], order[2]
    upper, lower = pl.ds(0, HALF_OUT), pl.ds(HALF_OUT, HALF_OUT)
    mine = out.at[core]
    add_core(0)
    ring = [
        links.start(mine.at[far, upper], out_in.at[0], at_z(1)),
        links.start(mine.at[far, lower], out_in.at[1], at_z(3)),
    ]
    add_core(1)
    add_core(2)
    ring += [
        links.start(mine.at[before, upper], out_in.at[2], at_z(3)),
        links.start(mine.at[after, lower], out_in.at[3], at_z(1)),
    ]
    relay_first(2)
    relay_first(3)
    add_core(3)
    for copy in gate_y:
        copy.wait_recv()
    gate_in[4] = gate_in[0] + gate_in[1] + gate_in[2] + gate_in[3]
    gate_x = [links.start(gate_in.at[4], gate_in.at[4 + step], at_x(step)) for step in (1, 2, 3)]

    for slot, target, rows, step in ((0, after, 0, 1), (1, before, HALF_OUT, 3)):
        ring[slot].wait_recv()

        def piece(index, carry, slot=slot, target=target, rows=rows):
            here = pl.ds(pl.multiple_of(index * 112, 16), 112)
            there = pl.ds(pl.multiple_of(index * 112 + rows, 16), 112)
            out_in[slot, here] = (wide(out_in[slot, here]) + wide(out[core, target, there])).astype(BF16)
            return carry

        lax.fori_loop(0, HALF_OUT // 112, piece, 0)
        ring.append(links.start(out_in.at[slot], out_in.at[4 + slot], at_z(step)))

    for number in range(4):
        end_first(number)
        send_second(number)
    for copy in gate_x:
        copy.wait_recv()
    gate_out[...] = gate_in[4] + gate_in[5] + gate_in[6] + gate_in[7]
    for number in range(4):
        relay_second(number)
    for half in range(2):
        ring[2 + half].wait_recv()
        ring[4 + half].wait_recv()

        def piece(index, carry, half=half):
            here = pl.ds(pl.multiple_of(index * 112, 16), 112)
            there = pl.ds(pl.multiple_of(index * 112 + half * HALF_OUT, 16), 112)
            total = wide(out[core, pz, there]) + wide(out_in[2 + half, here]) + wide(out_in[4 + half, here])
            layer_out[there, :] = total.astype(BF16)
            return carry

        lax.fori_loop(0, HALF_OUT // 112, piece, 0)
    for number in range(4):
        end_second(number)
    links.finish()


def reduce_all(attended, gated, cot_t, wout_t):
    tokens = attended.shape[0]
    vmem = pl.BlockSpec(memory_space=pltpu.VMEM)
    return pl.pallas_call(
        reduce_kernel,
        out_shape=(
            jax.ShapeDtypeStruct((4, GRAD_ROWS, 128), F32),
            jax.ShapeDtypeStruct((OUT_ROWS, tokens), BF16),
            jax.ShapeDtypeStruct((8, 128), F32),
        ),
        in_specs=[vmem] * 4,
        out_specs=(vmem,) * 3,
        scratch_shapes=[
            pltpu.VMEM((4, 4, 4, GRAD_ROWS, 128), BF16),
            pltpu.VMEM((4, 6, 2, GRAD_ROWS, 128), BF16),
            pltpu.VMEM((4, 4, GRAD_ROWS, 128), BF16),
            pltpu.VMEM((4, 6, SPLIT, 128), BF16),
            pltpu.VMEM((2, 4, OUT_ROWS, tokens), BF16),
            pltpu.VMEM((4, OUT_ROWS, tokens), BF16),
            pltpu.VMEM((6, HALF_OUT, tokens), BF16),
            pltpu.VMEM((4, 8, 128), F32),
            pltpu.VMEM((8, 8, 128), F32),
            pltpu.SemaphoreType.DMA((64,)),
            pltpu.SemaphoreType.DMA((64,)),
        ],
        compiler_params=pltpu.CompilerParams(
            collective_id=0, has_side_effects=True, vmem_limit_bytes=56 * 2**20
        ),
    )(attended, gated, cot_t, wout_t)


def shifted_2(value, axis, steps):
    count = lax.axis_size(axis)
    first, last = (max(0, -steps), min(count, count - steps))
    return lax.ppermute(value, axis, [(source, source + steps) for source in range(first, last)])


def hard_concrete(mask_logit, noise_draw):
    stretched = jax.nn.sigmoid(
        (jnp.log(noise_draw) - jnp.log(1.0 - noise_draw) + mask_logit) / BETA
    )
    shifted = stretched * (ZETA - GAMMA) + GAMMA
    gate_value = jnp.clip(shifted, 0.0, 1.0)
    inside = jnp.logical_and(shifted > 0.0, shifted < 1.0)
    gate_slope = jnp.where(inside, (ZETA - GAMMA) * stretched * (1.0 - stretched) / BETA, 0.0)
    expected = jax.nn.sigmoid(mask_logit - BETA * math.log(-GAMMA / ZETA))
    return (gate_value, gate_slope, PENALTY * expected * (1.0 - expected))


def body(tokens, norm_gain, w_query, w_key, value_weight, w_out, mask_logit, noise_draw, cotangent):
    tok_rows = tokens.shape[0]
    local_heads = mask_logit.shape[0]
    local_kv = w_key.shape[1] // HEAD_SIZE
    group_count_heads = local_heads // local_kv
    context = lax.axis_size("ctx")
    position = lax.axis_index("ctx")
    inv_root = 1.0 / math.sqrt(tok_rows * context)
    widened = tokens.astype(jnp.float32)
    moment = jnp.mean(jnp.square(widened), axis=1, keepdims=True)
    normed = (
        widened * lax.rsqrt(moment + EPSILON) * norm_gain.astype(jnp.float32)[None, :]
    ).astype(jnp.bfloat16)
    query_rows = jnp.dot(normed, w_query, preferred_element_type=jnp.float32).astype(jnp.bfloat16)
    rows_of_keys = jnp.dot(normed, w_key, preferred_element_type=jnp.float32).astype(jnp.bfloat16)
    rows_of_values = jnp.dot(normed, value_weight, preferred_element_type=jnp.float32).astype(
        jnp.bfloat16
    )
    reach = -(-WINDOW_TOKENS // tok_rows)
    earlier = []
    for distance in range(reach, 0, -1):
        earlier.append(shifted_2((rows_of_keys, rows_of_values), "ctx", distance))
    all_keys = jnp.concatenate([pair[0] for pair in earlier] + [rows_of_keys], axis=0)
    all_values = jnp.concatenate([pair[1] for pair in earlier] + [rows_of_values], axis=0)
    key_count = all_keys.shape[0]
    query_heads = query_rows.reshape(tok_rows, local_kv, group_count_heads, HEAD_SIZE)
    key_heads = all_keys.reshape(key_count, local_kv, HEAD_SIZE)
    value_heads = all_values.reshape(key_count, local_kv, HEAD_SIZE)
    scores = (
        jnp.einsum("rkgd,lkd->kgrl", query_heads, key_heads, preferred_element_type=jnp.float32)
        * SCORE_SCALE
    )
    query_pos = position * tok_rows + jnp.arange(tok_rows, dtype=jnp.int32)[:, None]
    key_pos = (position - reach) * tok_rows + jnp.arange(key_count, dtype=jnp.int32)[None, :]
    allowed = (key_pos <= query_pos) & (query_pos - key_pos < WINDOW_TOKENS) & (key_pos >= 0)
    scores = jnp.where(allowed, scores, -jnp.inf)
    row_max = jnp.max(scores, axis=-1, keepdims=True)
    lifted = jnp.exp(scores - row_max)
    prob_rows = (lifted / jnp.sum(lifted, axis=-1, keepdims=True)).astype(jnp.bfloat16)
    attended = jnp.einsum(
        "kgrl,lkd->rkgd", prob_rows, value_heads, preferred_element_type=jnp.float32
    )
    attended = attended.astype(jnp.bfloat16).reshape(tok_rows, local_heads * HEAD_SIZE)
    gate_value, gate_slope, penalty_term = hard_concrete(mask_logit, noise_draw)
    gate_columns = jnp.repeat(gate_value, HEAD_SIZE)
    gated = (attended.astype(jnp.float32) * gate_columns[None, :]).astype(jnp.bfloat16)
    grad_t, out_t, gate_rows = reduce_all(attended, gated, cotangent.T, w_out.T)
    layer_out = out_t.T
    summed = jnp.moveaxis(grad_t, 1, 2).reshape(local_heads * HEAD_SIZE, grad_t.shape[1])
    grad_out_proj = summed * gate_columns[:, None] * inv_root
    gate_product = jnp.sum(gate_rows[:local_heads], axis=1)
    grad_logit = gate_product * inv_root * gate_slope + penalty_term
    return (layer_out, grad_logit, grad_out_proj)


def solution(mesh):
    return jax.shard_map(
        body,
        mesh=mesh,
        in_specs=(
            P("ctx", None),
            P(),
            P(None, "head"),
            P(None, "head"),
            P(None, "head"),
            P("head", None),
            P("head"),
            P("head"),
            P("ctx", None),
        ),
        out_specs=(P("ctx", "head"), P("head"), P("head", "ctx")),
        check_vma=False,
    )
```

```python
import math

import jax
import jax.numpy as jnp
from jax import lax
from jax.experimental import pallas as pl
from jax.experimental.pallas import tpu as pltpu
from jax.sharding import PartitionSpec as P

HEAD_SIZE = 128


EPSILON = 1e-06
BETA = 2.0 / 3.0
GAMMA = -0.1
ZETA = 1.1
PENALTY = 0.1
SCORE_POWER = 168.0 ** (-0.5) * math.log2(math.e)


MESH = pl.DeviceIdType.MESH
BF16 = jnp.bfloat16
F32 = jnp.float32
GRAD_ROWS = 336
OUT_ROWS = 672
HALF_OUT = 336
SPLIT = 176


class Links:
    def __init__(self, send, recv):
        self.send, self.recv, self.count, self.open = send, recv, 0, []

    def start(self, source, target, device):
        copy = pltpu.make_async_remote_copy(
            src_ref=source,
            dst_ref=target,
            send_sem=self.send.at[self.count],
            recv_sem=self.recv.at[self.count],
            device_id=device,
            device_id_type=MESH,
        )
        self.count += 1
        copy.start()
        self.open.append(copy)
        return copy

    def finish(self):
        for copy in self.open:
            copy.wait_send()


def wide(value):
    return value.astype(F32)


def layer_kernel(
    tokens, gain, wq, wk, wv, wout, cot, gates,
    grad_out, layer_out, gate_out,
    rows_in, first_w, second_w, kv, relay, queries, top, low, acc, att, gated,
    grad, grad_in, line, line_in, out, out_core, out_in, gate_acc, gate_in, load, send, recv,
):
    ctx, head = lax.axis_index("ctx"), lax.axis_index("head")
    px, py = ctx // 4, ctx % 4
    pz, core = head // 2, head % 2

    def at_x(step):
        return ((px + step) % 4 * 4 + py, head)

    def at_y(step):
        return (px * 4 + (py + step) % 4, head)

    def at_z(step):
        return (ctx, (pz + step) % 4 * 2 + core)

    sibling = (ctx, pz * 2 + (1 - core))
    places = {"x": (px, at_x), "y": (py, at_y)}
    next_block = ((ctx + 1) % 16, head)
    two_on = ((px * 4 + (py + 1) % 4 + 2) % 16, head)
    back = (ctx + 14) % 16
    passer = (back // 4 * 4 + (back % 4 + 3) % 4, head)
    peers = [at(step) for at in (at_x, at_y) for step in (1, 2, 3)] + [at_z(1), at_z(3), sibling]
    peers += [((ctx + 15) % 16, head), passer]
    barrier = pltpu.get_barrier_semaphore()
    for peer in peers:
        pl.semaphore_signal(barrier, inc=1, device_id=peer, device_id_type=MESH)

    def fetch(number, source, target):
        copy = pltpu.make_async_copy(source, target, load.at[number])
        copy.start()
        return copy

    quarter = [pl.ds(128 * part, 128) for part in range(4)]
    token_loads = [fetch(part, tokens.at[rows], rows_in.at[rows]) for part, rows in enumerate(quarter)]
    key_load = fetch(4, wk, first_w.at[:, pl.ds(0, 256)])
    value_load = fetch(5, wv, first_w.at[:, pl.ds(256, 256)])
    query_load = fetch(6, wq, second_w)

    for part in range(4):
        token_loads[part].wait()

        def normalize(index, carry, part=part):
            rows = pl.ds(pl.multiple_of(part * 128 + index * 16, 16), 16)
            value = wide(rows_in[rows, :])
            moment = jnp.mean(value * value, axis=1, keepdims=True)
            rows_in[rows, :] = (value * lax.rsqrt(moment + EPSILON) * gain[...]).astype(BF16)
            return carry

        lax.fori_loop(0, 8, normalize, 0)

    links = Links(send, recv)
    key_load.wait()
    kv[0, 0] = jnp.dot(rows_in[...], first_w[:, 0:256], preferred_element_type=F32).astype(BF16)
    pl.semaphore_wait(barrier, len(peers))
    key_hop = links.start(kv.at[0, 0], kv.at[1, 0], next_block)
    value_load.wait()
    kv[0, 1] = jnp.dot(rows_in[...], first_w[:, 256:512], preferred_element_type=F32).astype(BF16)
    value_back = links.start(kv.at[0, 1], relay, at_y(3))
    value_hop = links.start(kv.at[0, 1], kv.at[1, 1], next_block)
    query_load.wait()
    queries[...] = jnp.dot(rows_in[...], second_w[...], preferred_element_type=F32).astype(BF16)

    strip = 768

    def cot_load(index):
        columns = pl.ds(pl.multiple_of(index * strip, 128), strip)
        return pltpu.make_async_copy(cot.at[:, columns], rows_in.at[:, columns], load.at[7 + index])

    def wout_load(index):
        columns = pl.ds(pl.multiple_of(index * strip, 128), strip)
        return pltpu.make_async_copy(wout.at[:, columns], rows_in.at[:, columns], load.at[14 + index])

    for index in range(7):
        cot_load(index).start()

    def attend(slot, pair):
        for half in range(2):
            rows = pl.ds(256 * half, 256)
            start, stop = (0, 256 * (half + 1)) if slot == 0 else (0, 512) if slot == 1 else (256 * half, 512)
            keys = kv[slot, 0, start:stop, 128 * pair : 128 * pair + 128]
            values = kv[slot, 1, start:stop, 128 * pair : 128 * pair + 128]
            for number in (2 * pair, 2 * pair + 1):
                here = pl.ds(128 * number, 128)
                scores = lax.dot_general(
                    queries[rows, here], keys, (((1,), (1,)), ((), ())), preferred_element_type=F32
                )
                if slot != 1:
                    row = lax.broadcasted_iota(jnp.int32, scores.shape, 0) + 256 * half
                    column = lax.broadcasted_iota(jnp.int32, scores.shape, 1) + start
                    allowed = column <= row if slot == 0 else column > row
                    scores = jnp.where(allowed, scores, -jnp.inf)
                peak = jnp.max(scores, axis=1, keepdims=True)
                if slot == 0:
                    lifted = jnp.exp2((scores - peak) * SCORE_POWER)
                    low[number, rows] = jnp.broadcast_to(jnp.sum(lifted, axis=1, keepdims=True), (256, 128))
                    acc[rows, here] = jnp.dot(lifted.astype(BF16), values, preferred_element_type=F32)
                    top[number, rows] = jnp.broadcast_to(peak, (256, 128))
                else:
                    before = top[number, rows]
                    peak = jnp.maximum(before, peak)
                    top[number, rows] = peak
                    fade = jnp.exp2((before - peak) * SCORE_POWER)
                    lifted = jnp.exp2((scores - peak[:, 0:1]) * SCORE_POWER)
                    low[number, rows] = low[number, rows] * fade + jnp.sum(lifted, axis=1, keepdims=True)
                    acc[rows, here] = acc[rows, here] * fade + jnp.dot(
                        lifted.astype(BF16), values, preferred_element_type=F32
                    )

    def close(pair):
        for number in (2 * pair, 2 * pair + 1):
            here = pl.ds(128 * number, 128)
            result = (acc[:, here] / low[number]).astype(BF16)
            att[:, here] = result
            gated[:, here] = (wide(result) * gates[:, here]).astype(BF16)

    attend(0, 0)
    attend(0, 1)
    key_hop.wait_recv()
    key_far = links.start(kv.at[1, 0], kv.at[2, 0], next_block)

    def turn_cot(index, carry):
        cot_load(index).wait()
        columns = pl.ds(pl.multiple_of(index * strip, 128), strip)
        second_w[columns, :] = rows_in[:, columns].T
        wout_load(index).start()
        return carry

    lax.fori_loop(0, 7, turn_cot, 0)
    value_back.wait_recv()
    value_far = links.start(relay, kv.at[2, 1], two_on)

    def turn_wout(index, carry):
        wout_load(index).wait()
        columns = pl.ds(pl.multiple_of(index * strip, 128), strip)
        first_w[columns, :] = rows_in[:, columns].T
        return carry

    lax.fori_loop(0, 7, turn_wout, 0)
    cot_t, wout_t = second_w, first_w

    def block_of(number, first, target, half):
        if first == "y":
            return grad.at[number, pl.ds(2 * half, 2), target]
        return grad.at[number, target, pl.ds(2 * half, 2)]

    firsts = ["y", "x", "y", "x"]
    gate_acc[...] = jnp.zeros_like(gate_acc)
    gate_in[0] = jnp.zeros((8, 128), F32)
    tall = 4 * GRAD_ROWS

    def grad_pair(pair):
        def chunk(index, carry):
            rows = pl.ds(pl.multiple_of(index * tall, 16), tall)
            product = jnp.dot(
                cot_t[rows, :], att[:, 256 * pair : 256 * pair + 256], preferred_element_type=F32
            )
            for side in range(2):
                number = 2 * pair + side
                mine = product[:, 128 * side : 128 * side + 128]
                grad[number, index] = mine.astype(BF16).reshape(4, GRAD_ROWS, 128)
                weighed = mine * wide(wout_t[rows, 128 * number : 128 * number + 128])
                gate_acc[number] += jnp.sum(weighed.reshape(tall // 8, 8, 128), axis=0)
            return carry

        lax.fori_loop(0, 4, chunk, 0)

    stage1 = {}

    def send_first(number):
        first = firsts[number]
        place, at = places[first]
        far, after, before = (place + 2) % 4, (place + 1) % 4, (place + 3) % 4
        box = grad_in.at[number]
        stage1[number] = [
            links.start(block_of(number, first, far, 0), box.at[0], at(1)),
            links.start(block_of(number, first, far, 1), box.at[1], at(3)),
            links.start(block_of(number, first, before, 0), box.at[2], at(3)),
            links.start(block_of(number, first, after, 1), box.at[3], at(1)),
        ]

    def relay_first(number):
        first = firsts[number]
        place, at = places[first]
        after, before = (place + 1) % 4, (place + 3) % 4
        box = grad_in.at[number]
        for slot, target, half, step in ((0, after, 0, 1), (1, before, 1, 3)):
            stage1[number][slot].wait_recv()
            box[slot] = (wide(box[slot]) + wide(block_of(number, first, target, half)[...])).astype(BF16)
            stage1[number].append(links.start(box.at[slot], box.at[4 + slot], at(step)))

    def end_first(number):
        first = firsts[number]
        place, _ = places[first]
        box = grad_in.at[number]
        for half in range(2):
            stage1[number][2 + half].wait_recv()
            stage1[number][4 + half].wait_recv()
            total = wide(block_of(number, first, place, half)[...]) + wide(box[2 + half]) + wide(box[4 + half])
            line[number, pl.ds(2 * half, 2)] = total.astype(BF16)

    stage2 = {}
    cuts = (pl.ds(0, SPLIT), pl.ds(SPLIT, GRAD_ROWS - SPLIT))
    sizes = (pl.ds(0, SPLIT), pl.ds(0, GRAD_ROWS - SPLIT))

    def send_second(number):
        place, at = places["x" if firsts[number] == "y" else "y"]
        far, after, before = (place + 2) % 4, (place + 1) % 4, (place + 3) % 4
        mine, box = line.at[number], line_in.at[number]
        stage2[number] = [
            links.start(mine.at[far, cuts[0]], box.at[0, sizes[0]], at(1)),
            links.start(mine.at[far, cuts[1]], box.at[1, sizes[1]], at(3)),
            links.start(mine.at[before, cuts[0]], box.at[2, sizes[0]], at(3)),
            links.start(mine.at[after, cuts[1]], box.at[3, sizes[1]], at(1)),
        ]

    def relay_second(number):
        place, at = places["x" if firsts[number] == "y" else "y"]
        after, before = (place + 1) % 4, (place + 3) % 4
        mine, box = line.at[number], line_in.at[number]
        for slot, target, step in ((0, after, 1), (1, before, 3)):
            stage2[number][slot].wait_recv()
            part = box.at[slot, sizes[slot]]
            part[...] = (wide(part[...]) + wide(mine[target, cuts[slot]])).astype(BF16)
            stage2[number].append(links.start(part, box.at[4 + slot, sizes[slot]], at(step)))

    def end_second(number):
        place, _ = places["x" if firsts[number] == "y" else "y"]
        mine, box = line.at[number], line_in.at[number]
        for half in range(2):
            stage2[number][2 + half].wait_recv()
            stage2[number][4 + half].wait_recv()
            grad_out[number, cuts[half]] = (
                wide(mine[place, cuts[half]])
                + wide(box[2 + half, sizes[half]])
                + wide(box[4 + half, sizes[half]])
            )

    across = []

    def out_part(place):
        rows = pl.ds(pl.multiple_of(place * (2 * OUT_ROWS), 16), 2 * OUT_ROWS)
        product = lax.dot_general(
            wout_t[rows, :], gated[...], (((1,), (1,)), ((), ())), preferred_element_type=F32
        ).astype(BF16)
        out[place] = product.reshape(2, OUT_ROWS, 512)
        across.append(links.start(out.at[place, 1 - core], out_core.at[place], sibling))

    key_hop_done = value_hop
    key_hop_done.wait_recv()

    @pl.when(ctx >= 1)
    def _():
        attend(1, 0)
        attend(1, 1)

    key_far.wait_recv()
    value_far.wait_recv()

    @pl.when(ctx >= 2)
    def _():
        attend(2, 0)

    close(0)
    grad_pair(0)
    send_first(0)
    send_first(1)

    @pl.when(ctx >= 2)
    def _():
        attend(2, 1)

    close(1)
    order = [(pz + step) % 4 for step in (2, 1, 3, 0)]
    for place in order:
        out_part(place)
    relay_first(0)
    relay_first(1)
    grad_pair(1)
    send_first(2)
    send_first(3)

    for number in range(4):
        gate_in[0, pl.ds(number, 1)] = jnp.sum(gate_acc[number], axis=0, keepdims=True)
    gate_y = [links.start(gate_in.at[0], gate_in.at[step], at_y(step)) for step in (1, 2, 3)]

    def add_core(index):
        across[index].wait_recv()
        place = order[index]

        def piece(step, carry):
            rows = pl.ds(pl.multiple_of(step * 112, 16), 112)
            out_core[place, rows] = (wide(out[place, core, rows]) + wide(out_core[place, rows])).astype(BF16)
            return carry

        lax.fori_loop(0, OUT_ROWS // 112, piece, 0)

    far, after, before = order[0], order[1], order[2]
    upper, lower = pl.ds(0, HALF_OUT), pl.ds(HALF_OUT, HALF_OUT)
    add_core(0)
    ring = [
        links.start(out_core.at[far, upper], out_in.at[0], at_z(1)),
        links.start(out_core.at[far, lower], out_in.at[1], at_z(3)),
    ]
    add_core(1)
    add_core(2)
    ring += [
        links.start(out_core.at[before, upper], out_in.at[2], at_z(3)),
        links.start(out_core.at[after, lower], out_in.at[3], at_z(1)),
    ]
    for number in (0, 1):
        end_first(number)
        send_second(number)
    add_core(3)
    relay_first(2)
    relay_first(3)
    for slot, target, rows, step in ((0, after, 0, 1), (1, before, HALF_OUT, 3)):
        ring[slot].wait_recv()

        def piece(index, carry, slot=slot, target=target, rows=rows):
            here = pl.ds(pl.multiple_of(index * 112, 16), 112)
            there = pl.ds(pl.multiple_of(index * 112 + rows, 16), 112)
            out_in[slot, here] = (wide(out_in[slot, here]) + wide(out_core[target, there])).astype(BF16)
            return carry

        lax.fori_loop(0, HALF_OUT // 112, piece, 0)
        ring.append(links.start(out_in.at[slot], out_in.at[4 + slot], at_z(step)))

    relay_second(0)
    relay_second(1)
    for copy in gate_y:
        copy.wait_recv()
    gate_in[4] = gate_in[0] + gate_in[1] + gate_in[2] + gate_in[3]
    gate_x = [links.start(gate_in.at[4], gate_in.at[4 + step], at_x(step)) for step in (1, 2, 3)]
    for number in (2, 3):
        end_first(number)
        send_second(number)
    end_second(0)
    end_second(1)
    for copy in gate_x:
        copy.wait_recv()
    gate_out[...] = gate_in[4] + gate_in[5] + gate_in[6] + gate_in[7]
    relay_second(2)
    relay_second(3)
    for half in range(2):
        ring[2 + half].wait_recv()
        ring[4 + half].wait_recv()

        def piece(index, carry, half=half):
            here = pl.ds(pl.multiple_of(index * 112, 16), 112)
            there = pl.ds(pl.multiple_of(index * 112 + half * HALF_OUT, 16), 112)
            total = wide(out_core[pz, there]) + wide(out_in[2 + half, here]) + wide(out_in[4 + half, here])
            layer_out[there, :] = total.astype(BF16)
            return carry

        lax.fori_loop(0, HALF_OUT // 112, piece, 0)
    end_second(2)
    end_second(3)
    links.finish()


def run_layer(tokens, gain, wq, wk, wv, wout, cot, gates):
    vmem = pl.BlockSpec(memory_space=pltpu.VMEM)
    hbm = pl.BlockSpec(memory_space=pl.ANY)
    wide_w = pltpu.VMEM((5376, 512), BF16)
    return pl.pallas_call(
        layer_kernel,
        out_shape=(
            jax.ShapeDtypeStruct((4, GRAD_ROWS, 128), F32),
            jax.ShapeDtypeStruct((OUT_ROWS, 512), BF16),
            jax.ShapeDtypeStruct((8, 128), F32),
        ),
        in_specs=[hbm, vmem, hbm, hbm, hbm, hbm, hbm, vmem],
        out_specs=(vmem,) * 3,
        scratch_shapes=[
            pltpu.VMEM((512, 5376), BF16),
            wide_w,
            wide_w,
            pltpu.VMEM((3, 2, 512, 256), BF16),
            pltpu.VMEM((512, 256), BF16),
            pltpu.VMEM((512, 512), BF16),
            pltpu.VMEM((4, 512, 128), F32),
            pltpu.VMEM((4, 512, 128), F32),
            pltpu.VMEM((512, 512), F32),
            pltpu.VMEM((512, 512), BF16),
            pltpu.VMEM((512, 512), BF16),
            pltpu.VMEM((4, 4, 4, GRAD_ROWS, 128), BF16),
            pltpu.VMEM((4, 6, 2, GRAD_ROWS, 128), BF16),
            pltpu.VMEM((4, 4, GRAD_ROWS, 128), BF16),
            pltpu.VMEM((4, 6, SPLIT, 128), BF16),
            pltpu.VMEM((4, 2, OUT_ROWS, 512), BF16),
            pltpu.VMEM((4, OUT_ROWS, 512), BF16),
            pltpu.VMEM((6, HALF_OUT, 512), BF16),
            pltpu.VMEM((4, 8, 128), F32),
            pltpu.VMEM((8, 8, 128), F32),
            pltpu.SemaphoreType.DMA((21,)),
            pltpu.SemaphoreType.DMA((69,)),
            pltpu.SemaphoreType.DMA((69,)),
        ],
        compiler_params=pltpu.CompilerParams(
            collective_id=0, has_side_effects=True, vmem_limit_bytes=58 * 2**20
        ),
    )(tokens, gain, wq, wk, wv, wout, cot, gates)


def hard_concrete(mask_logit, noise_draw):
    stretched = jax.nn.sigmoid(
        (jnp.log(noise_draw) - jnp.log(1.0 - noise_draw) + mask_logit) / BETA
    )
    shifted = stretched * (ZETA - GAMMA) + GAMMA
    gate_value = jnp.clip(shifted, 0.0, 1.0)
    inside = jnp.logical_and(shifted > 0.0, shifted < 1.0)
    gate_slope = jnp.where(inside, (ZETA - GAMMA) * stretched * (1.0 - stretched) / BETA, 0.0)
    expected = jax.nn.sigmoid(mask_logit - BETA * math.log(-GAMMA / ZETA))
    return (gate_value, gate_slope, PENALTY * expected * (1.0 - expected))


def body(tokens, norm_gain, w_query, w_key, value_weight, w_out, mask_logit, noise_draw, cotangent):
    local_heads = mask_logit.shape[0]
    inv_root = 1.0 / math.sqrt(tokens.shape[0] * lax.axis_size("ctx"))
    gate_value, gate_slope, penalty_term = hard_concrete(mask_logit, noise_draw)
    gate_columns = jnp.repeat(gate_value, HEAD_SIZE)
    grad_t, out_t, gate_rows = run_layer(
        tokens, norm_gain.astype(F32)[None, :], w_query, w_key, value_weight, w_out, cotangent, gate_columns[None, :]
    )
    layer_out = out_t.T
    summed = jnp.moveaxis(grad_t, 1, 2).reshape(local_heads * HEAD_SIZE, grad_t.shape[1])
    grad_out_proj = summed * gate_columns[:, None] * inv_root
    gate_product = jnp.sum(gate_rows[:local_heads], axis=1)
    grad_logit = gate_product * inv_root * gate_slope + penalty_term
    return (layer_out, grad_logit, grad_out_proj)


def solution(mesh):
    return jax.shard_map(
        body,
        mesh=mesh,
        in_specs=(
            P("ctx", None),
            P(),
            P(None, "head"),
            P(None, "head"),
            P(None, "head"),
            P("head", None),
            P("head"),
            P("head"),
            P("ctx", None),
        ),
        out_specs=(P("ctx", "head"), P("head"), P("head", "ctx")),
        check_vma=False,
    )
```

```python
import math

import jax
import jax.numpy as jnp
from jax import lax
from jax.experimental import pallas as pl
from jax.experimental.pallas import tpu as pltpu
from jax.sharding import PartitionSpec as P

HEAD_SIZE = 128


EPSILON = 1e-06
BETA = 2.0 / 3.0
GAMMA = -0.1
ZETA = 1.1
PENALTY = 0.1
SCORE_POWER = 168.0 ** (-0.5) * math.log2(math.e)


MESH = pl.DeviceIdType.MESH
BF16 = jnp.bfloat16
F32 = jnp.float32
GRAD_ROWS = 336
OUT_ROWS = 672
HALF_OUT = 336
SPLIT = 176
INV_ROOT = 1.0 / math.sqrt(8192)


def hard_concrete(mask_logit, noise_draw):
    stretched = jax.nn.sigmoid(
        (jnp.log(noise_draw) - jnp.log(1.0 - noise_draw) + mask_logit) / BETA
    )
    shifted = stretched * (ZETA - GAMMA) + GAMMA
    gate_value = jnp.clip(shifted, 0.0, 1.0)
    inside = jnp.logical_and(shifted > 0.0, shifted < 1.0)
    gate_slope = jnp.where(inside, (ZETA - GAMMA) * stretched * (1.0 - stretched) / BETA, 0.0)
    expected = jax.nn.sigmoid(mask_logit - BETA * math.log(-GAMMA / ZETA))
    return (gate_value, gate_slope, PENALTY * expected * (1.0 - expected))


class Links:
    def __init__(self, send, recv):
        self.send, self.recv, self.count, self.open = send, recv, 0, []

    def start(self, source, target, device):
        copy = pltpu.make_async_remote_copy(
            src_ref=source,
            dst_ref=target,
            send_sem=self.send.at[self.count],
            recv_sem=self.recv.at[self.count],
            device_id=device,
            device_id_type=MESH,
        )
        self.count += 1
        copy.start()
        self.open.append(copy)
        return copy

    def finish(self):
        for copy in self.open:
            copy.wait_send()


def wide(value):
    return value.astype(F32)


def layer_kernel(
    tokens, gain, wq, wk, wv, wout, mask_logit, noise_draw, cot,
    layer_out, gate_out, grad_out,
    rows_in, cot_in, first_w, second_w, scale, keys_at, values_at, relay_k, relay_v, queries, top, low, acc, att, gated,
    grad, grad_in, line, line_in, out, out_core, out_in, gate_acc, gate_in, load, send, recv,
):
    ctx, head = lax.axis_index("ctx"), lax.axis_index("head")
    px, py = ctx // 4, ctx % 4
    pz, core = head // 2, head % 2

    def at_x(step):
        return ((px + step) % 4 * 4 + py, head)

    def at_y(step):
        return (px * 4 + (py + step) % 4, head)

    def at_z(step):
        return (ctx, (pz + step) % 4 * 2 + core)

    sibling = (ctx, pz * 2 + (1 - core))
    places = {"x": (px, at_x), "y": (py, at_y)}
    next_block = ((ctx + 1) % 16, head)
    two_on = ((px * 4 + (py + 1) % 4 + 2) % 16, head)
    back = (ctx + 14) % 16
    passer = (back // 4 * 4 + (back % 4 + 3) % 4, head)
    peers = [at(step) for at in (at_x, at_y) for step in (1, 2, 3)] + [at_z(1), at_z(3), sibling]
    peers += [((ctx + 15) % 16, head), passer]
    barrier = pltpu.get_barrier_semaphore()
    for peer in peers:
        pl.semaphore_signal(barrier, inc=1, device_id=peer, device_id_type=MESH)

    def fetch(number, source, target):
        copy = pltpu.make_async_copy(source, target, load.at[number])
        copy.start()
        return copy

    quarter = [pl.ds(128 * part, 128) for part in range(4)]
    token_loads = [fetch(part, tokens.at[rows], rows_in.at[rows]) for part, rows in enumerate(quarter)]
    weight_loads = []
    weight_copies = [
        (4, wk.at[:, pl.ds(0, 128)], first_w.at[:, pl.ds(0, 128)]),
        (5, wv.at[:, pl.ds(0, 128)], first_w.at[:, pl.ds(128, 128)]),
        (6, wk.at[:, pl.ds(128, 128)], first_w.at[:, pl.ds(256, 128)]),
        (7, wv.at[:, pl.ds(128, 128)], first_w.at[:, pl.ds(384, 128)]),
        (8, wq, second_w),
    ]

    strip = 768

    def cot_load(index):
        columns = pl.ds(pl.multiple_of(index * strip, 128), strip)
        return pltpu.make_async_copy(cot.at[:, columns], cot_in.at[:, columns], load.at[9 + index])

    def wout_load(index):
        columns = pl.ds(pl.multiple_of(index * strip, 128), strip)
        return pltpu.make_async_copy(wout.at[:, columns], rows_in.at[:, columns], load.at[16 + index])

    for part in range(4):
        token_loads[part].wait()
        for copy in weight_copies[0:2] if part == 0 else weight_copies[2:4] if part == 2 else weight_copies[4:] if part == 3 else []:
            weight_loads.append(fetch(*copy))

        def weigh(index, carry, part=part):
            rows = pl.ds(pl.multiple_of(part * 128 + index * 32, 32), 32)
            total = jnp.zeros((32, 128), F32)
            for tile in range(42):
                columns = slice(128 * tile, 128 * tile + 128)
                value = rows_in[rows, columns]
                total += wide(value) * wide(value)
                rows_in[rows, columns] = value * gain[columns][None, :]
            scale[rows, :] = total
            return carry

        lax.fori_loop(0, 4, weigh, 0)

    for index in range(7):
        cot_load(index).start()
    moment = jnp.sum(scale[...], axis=1, keepdims=True) * (1.0 / 5376)
    scale[...] = jnp.broadcast_to(lax.rsqrt(moment + EPSILON), (512, 128))

    def project(weight):
        product = jnp.dot(rows_in[...], weight, preferred_element_type=F32)
        return (product * jnp.concatenate([scale[...]] * (weight.shape[1] // 128), axis=1)).astype(BF16)

    links = Links(send, recv)

    def keys_and_values(pair):
        for copy in weight_loads[2 * pair : 2 * pair + 2]:
            copy.wait()
        both = project(first_w[:, 256 * pair : 256 * pair + 256])
        keys_at[0, pair] = both[:, 0:128]
        values_at[0, pair] = both[:, 128:256].T

    def pass_on(sources, targets, device):
        return [links.start(source, target, device) for source, target in zip(sources, targets)]

    def arrive(copies):
        for copy in copies:
            copy.wait_recv()

    def held(slot, pair):
        return keys_at.at[slot, pair], values_at.at[slot, pair]

    keys_and_values(0)
    pl.semaphore_wait(barrier, len(peers))
    hop0 = pass_on(held(0, 0), held(1, 0), next_block)
    keys_and_values(1)
    back1 = pass_on(held(0, 1), (relay_k, relay_v), at_y(3))
    hop1 = pass_on(held(0, 1), held(1, 1), next_block)
    weight_loads[4].wait()
    queries[...] = project(second_w[...])

    for index in range(7):
        wout_load(index).start()

    def attend(slot, pair):
        for block in range(4):
            rows = pl.ds(128 * block, 128)
            start, stop = (0, 128 * (block + 1)) if slot == 0 else (0, 512) if slot == 1 else (128 * block, 512)
            keys = keys_at[slot, pair, start:stop, :]
            values = values_at[slot, pair, :, start:stop]
            for number in (2 * pair, 2 * pair + 1):
                here, one = pl.ds(128 * number, 128), pl.ds(number, 1)
                scores = lax.dot_general(
                    keys, queries[rows, here], (((1,), (1,)), ((), ())), preferred_element_type=F32
                )
                if slot != 1:
                    key = lax.broadcasted_iota(jnp.int32, scores.shape, 0) + start
                    query = lax.broadcasted_iota(jnp.int32, scores.shape, 1) + 128 * block
                    scores = jnp.where(key <= query if slot == 0 else key > query, scores, -jnp.inf)
                peak = jnp.max(scores, axis=0, keepdims=True)
                if slot > 0:
                    before = top[one, rows]
                    peak = jnp.maximum(before, peak)
                    fade = jnp.exp2((before - peak) * SCORE_POWER)
                lifted = jnp.exp2((scores - peak) * SCORE_POWER)
                total = jnp.sum(lifted, axis=0, keepdims=True)
                mixed = jnp.dot(values, lifted.astype(BF16), preferred_element_type=F32)
                top[one, rows] = peak
                if slot > 0:
                    low[one, rows] = low[one, rows] * fade + total
                    acc[here, rows] = acc[here, rows] * fade + mixed
                else:
                    low[one, rows] = total
                    acc[here, rows] = mixed

    def close(pair):
        for number in (2 * pair, 2 * pair + 1):
            here = pl.ds(128 * number, 128)
            result = (acc[here, :] * (1.0 / low[pl.ds(number, 1), :])).astype(BF16)
            att[here, :] = result
            gated[here, :] = (wide(result) * gates[number][0:1, 0:1]).astype(BF16)

    gates, slopes, penalties = zip(
        *(
            hard_concrete(jnp.full((8, 128), mask_logit[number], F32), jnp.full((8, 128), noise_draw[number], F32))
            for number in range(4)
        )
    )
    attend(0, 0)
    attend(0, 1)
    arrive(hop0)
    far0 = pass_on(held(1, 0), held(2, 0), next_block)

    def turn_cot(index, carry):
        cot_load(index).wait()
        columns = pl.ds(pl.multiple_of(index * strip, 128), strip)
        second_w[columns, :] = cot_in[:, columns].T
        return carry

    lax.fori_loop(0, 7, turn_cot, 0)
    arrive(back1)
    far1 = pass_on((relay_k, relay_v), held(2, 1), two_on)

    @pl.when(ctx >= 1)
    def _():
        attend(1, 0)

    def turn_wout(index, carry):
        wout_load(index).wait()
        columns = pl.ds(pl.multiple_of(index * strip, 128), strip)
        first_w[columns, :] = rows_in[:, columns].T
        return carry

    lax.fori_loop(0, 7, turn_wout, 0)
    cot_t, wout_t = second_w, first_w

    def block_of(number, first, target, half):
        if first == "y":
            return grad.at[number, pl.ds(2 * half, 2), target]
        return grad.at[number, target, pl.ds(2 * half, 2)]

    firsts = ["y", "x", "y", "x"]
    gate_acc[...] = jnp.zeros_like(gate_acc)
    gate_in[0] = jnp.zeros((8, 128), F32)
    tall = 4 * GRAD_ROWS

    def grad_pair(pair):
        def chunk(index, carry):
            rows = pl.ds(pl.multiple_of(index * tall, 16), tall)
            product = lax.dot_general(
                cot_t[rows, :], att[256 * pair : 256 * pair + 256, :], (((1,), (1,)), ((), ())),
                preferred_element_type=F32,
            )
            for side in range(2):
                number = 2 * pair + side
                mine = product[:, 128 * side : 128 * side + 128]
                grad[number, index] = mine.astype(BF16).reshape(4, GRAD_ROWS, 128)
                weighed = mine * wide(wout_t[rows, 128 * number : 128 * number + 128])
                gate_acc[number] += jnp.sum(weighed.reshape(tall // 8, 8, 128), axis=0)
            return carry

        lax.fori_loop(0, 4, chunk, 0)

    stage1 = {}

    def send_first(number):
        first = firsts[number]
        place, at = places[first]
        far, after, before = (place + 2) % 4, (place + 1) % 4, (place + 3) % 4
        box = grad_in.at[number]
        stage1[number] = [
            links.start(block_of(number, first, far, 0), box.at[0], at(1)),
            links.start(block_of(number, first, far, 1), box.at[1], at(3)),
            links.start(block_of(number, first, before, 0), box.at[2], at(3)),
            links.start(block_of(number, first, after, 1), box.at[3], at(1)),
        ]

    def relay_first(number):
        first = firsts[number]
        place, at = places[first]
        after, before = (place + 1) % 4, (place + 3) % 4
        box = grad_in.at[number]
        for slot, target, half, step in ((0, after, 0, 1), (1, before, 1, 3)):
            stage1[number][slot].wait_recv()
            box[slot] = (wide(box[slot]) + wide(block_of(number, first, target, half)[...])).astype(BF16)
            stage1[number].append(links.start(box.at[slot], box.at[4 + slot], at(step)))

    def end_first(number):
        first = firsts[number]
        place, _ = places[first]
        box = grad_in.at[number]
        for half in range(2):
            stage1[number][2 + half].wait_recv()
            stage1[number][4 + half].wait_recv()
            total = wide(block_of(number, first, place, half)[...]) + wide(box[2 + half]) + wide(box[4 + half])
            line[number, pl.ds(2 * half, 2)] = total.astype(BF16)

    stage2 = {}
    cuts = (pl.ds(0, SPLIT), pl.ds(SPLIT, GRAD_ROWS - SPLIT))
    sizes = (pl.ds(0, SPLIT), pl.ds(0, GRAD_ROWS - SPLIT))

    def send_second(number):
        place, at = places["x" if firsts[number] == "y" else "y"]
        far, after, before = (place + 2) % 4, (place + 1) % 4, (place + 3) % 4
        mine, box = line.at[number], line_in.at[number]
        stage2[number] = [
            links.start(mine.at[far, cuts[0]], box.at[0, sizes[0]], at(1)),
            links.start(mine.at[far, cuts[1]], box.at[1, sizes[1]], at(3)),
            links.start(mine.at[before, cuts[0]], box.at[2, sizes[0]], at(3)),
            links.start(mine.at[after, cuts[1]], box.at[3, sizes[1]], at(1)),
        ]

    def relay_second(number):
        place, at = places["x" if firsts[number] == "y" else "y"]
        after, before = (place + 1) % 4, (place + 3) % 4
        mine, box = line.at[number], line_in.at[number]
        for slot, target, step in ((0, after, 1), (1, before, 3)):
            stage2[number][slot].wait_recv()
            part = box.at[slot, sizes[slot]]
            part[...] = (wide(part[...]) + wide(mine[target, cuts[slot]])).astype(BF16)
            stage2[number].append(links.start(part, box.at[4 + slot, sizes[slot]], at(step)))

    def end_second(number):
        place, _ = places["x" if firsts[number] == "y" else "y"]
        mine, box = line.at[number], line_in.at[number]
        for half in range(2):
            stage2[number][2 + half].wait_recv()
            stage2[number][4 + half].wait_recv()
            total = (
                wide(mine[place, cuts[half]])
                + wide(box[2 + half, sizes[half]])
                + wide(box[4 + half, sizes[half]])
            )
            grad_out[cuts[half], 128 * number : 128 * number + 128] = total * (gates[number][0:1, 0:1] * INV_ROOT)

    across = []

    def out_part(place):
        rows = pl.ds(pl.multiple_of(place * (2 * OUT_ROWS), 16), 2 * OUT_ROWS)
        product = jnp.dot(wout_t[rows, :], gated[...], preferred_element_type=F32).astype(BF16)
        out[place] = product.reshape(2, OUT_ROWS, 512)
        across.append(links.start(out.at[place, 1 - core], out_core.at[place], sibling))

    arrive(far0)

    @pl.when(ctx >= 2)
    def _():
        attend(2, 0)

    close(0)
    grad_pair(0)
    send_first(0)
    send_first(1)
    arrive(hop1)

    @pl.when(ctx >= 1)
    def _():
        attend(1, 1)

    arrive(far1)

    @pl.when(ctx >= 2)
    def _():
        attend(2, 1)

    close(1)
    order = [(pz + step) % 4 for step in (2, 1, 3, 0)]
    for place in order[:3]:
        out_part(place)

    def add_core(index):
        across[index].wait_recv()
        place = order[index]

        def piece(step, carry):
            rows = pl.ds(pl.multiple_of(step * 112, 16), 112)
            out_core[place, rows] = (wide(out[place, core, rows]) + wide(out_core[place, rows])).astype(BF16)
            return carry

        lax.fori_loop(0, OUT_ROWS // 112, piece, 0)

    far, after, before = order[0], order[1], order[2]
    upper, lower = pl.ds(0, HALF_OUT), pl.ds(HALF_OUT, HALF_OUT)
    add_core(0)
    ring = [
        links.start(out_core.at[far, upper], out_in.at[0], at_z(1)),
        links.start(out_core.at[far, lower], out_in.at[1], at_z(3)),
    ]
    relay_first(0)
    relay_first(1)
    grad_pair(1)
    send_first(2)
    send_first(3)
    add_core(1)
    add_core(2)
    ring += [
        links.start(out_core.at[before, upper], out_in.at[2], at_z(3)),
        links.start(out_core.at[after, lower], out_in.at[3], at_z(1)),
    ]

    out_part(order[3])

    for number in range(4):
        gate_in[0, pl.ds(number, 1)] = jnp.sum(gate_acc[number], axis=0, keepdims=True)
    gate_y = [links.start(gate_in.at[0], gate_in.at[step], at_y(step)) for step in (1, 2, 3)]
    add_core(3)
    for number in (0, 1):
        end_first(number)
        send_second(number)
    relay_first(2)
    relay_first(3)
    for slot, target, rows, step in ((0, after, 0, 1), (1, before, HALF_OUT, 3)):
        ring[slot].wait_recv()

        def piece(index, carry, slot=slot, target=target, rows=rows):
            here = pl.ds(pl.multiple_of(index * 112, 16), 112)
            there = pl.ds(pl.multiple_of(index * 112 + rows, 16), 112)
            out_in[slot, here] = (wide(out_in[slot, here]) + wide(out_core[target, there])).astype(BF16)
            return carry

        lax.fori_loop(0, HALF_OUT // 112, piece, 0)
        ring.append(links.start(out_in.at[slot], out_in.at[4 + slot], at_z(step)))

    for copy in gate_y:
        copy.wait_recv()
    gate_in[4] = gate_in[0] + gate_in[1] + gate_in[2] + gate_in[3]
    gate_x = [links.start(gate_in.at[4], gate_in.at[4 + step], at_x(step)) for step in (1, 2, 3)]
    relay_second(0)
    relay_second(1)
    for number in (2, 3):
        end_first(number)
        send_second(number)
    end_second(0)
    end_second(1)
    for copy in gate_x:
        copy.wait_recv()
    gate_sum = gate_in[4] + gate_in[5] + gate_in[6] + gate_in[7]
    for number in range(4):
        product = jnp.sum(gate_sum[number : number + 1, :], axis=1, keepdims=True)
        answer = product * INV_ROOT * slopes[number] + penalties[number]
        gate_out[pl.ds(number, 1), :] = jnp.broadcast_to(answer[0:1, :], (1, 128))
    relay_second(2)
    relay_second(3)
    for half in range(2):
        ring[2 + half].wait_recv()
        ring[4 + half].wait_recv()

        def piece(index, carry, half=half):
            here = pl.ds(pl.multiple_of(index * 112, 16), 112)
            there = pl.ds(pl.multiple_of(index * 112 + half * HALF_OUT, 16), 112)
            total = wide(out_core[pz, there]) + wide(out_in[2 + half, here]) + wide(out_in[4 + half, here])
            layer_out[there, :] = total.astype(BF16)
            return carry

        lax.fori_loop(0, HALF_OUT // 112, piece, 0)
    end_second(2)
    end_second(3)
    links.finish()


def deliver_kernel(layer_in, gate_in, grad_in, layer_out, gate_out, grad_out):
    layer_out[...] = layer_in[...]
    grad_out[...] = grad_in[...]
    for number in range(4):
        gate_out[number] = gate_in[number, 0]


def body(*args):
    vmem = pl.BlockSpec(memory_space=pltpu.VMEM)
    smem = pl.BlockSpec(memory_space=pltpu.SMEM)
    hbm = pl.BlockSpec(memory_space=pl.ANY)
    wide_w = pltpu.VMEM((5376, 512), BF16)
    tokens, norm_gain, *rest = args
    layer_shape = jax.ShapeDtypeStruct((OUT_ROWS, 512), BF16)
    grad_shape = jax.ShapeDtypeStruct((GRAD_ROWS, 512), F32)
    results = pl.pallas_call(
        layer_kernel,
        out_shape=(layer_shape, jax.ShapeDtypeStruct((8, 128), F32), grad_shape),
        in_specs=[hbm, vmem, hbm, hbm, hbm, hbm, smem, smem, hbm],
        out_specs=(vmem,) * 3,
        scratch_shapes=[
            pltpu.VMEM((512, 5376), BF16),
            pltpu.VMEM((512, 5376), BF16),
            wide_w,
            wide_w,
            pltpu.VMEM((512, 128), F32),
            pltpu.VMEM((3, 2, 512, 128), BF16),
            pltpu.VMEM((3, 2, 128, 512), BF16),
            pltpu.VMEM((512, 128), BF16),
            pltpu.VMEM((128, 512), BF16),
            pltpu.VMEM((512, 512), BF16),
            pltpu.VMEM((8, 512), F32),
            pltpu.VMEM((8, 512), F32),
            pltpu.VMEM((512, 512), F32),
            pltpu.VMEM((512, 512), BF16),
            pltpu.VMEM((512, 512), BF16),
            pltpu.VMEM((4, 4, 4, GRAD_ROWS, 128), BF16),
            pltpu.VMEM((4, 6, 2, GRAD_ROWS, 128), BF16),
            pltpu.VMEM((4, 4, GRAD_ROWS, 128), BF16),
            pltpu.VMEM((4, 6, SPLIT, 128), BF16),
            pltpu.VMEM((4, 2, OUT_ROWS, 512), BF16),
            pltpu.VMEM((4, OUT_ROWS, 512), BF16),
            pltpu.VMEM((6, HALF_OUT, 512), BF16),
            pltpu.VMEM((4, 8, 128), F32),
            pltpu.VMEM((8, 8, 128), F32),
            pltpu.SemaphoreType.DMA((23,)),
            pltpu.SemaphoreType.DMA((74,)),
            pltpu.SemaphoreType.DMA((74,)),
        ],
        compiler_params=pltpu.CompilerParams(
            collective_id=0, has_side_effects=True, vmem_limit_bytes=58 * 2**20
        ),
    )(tokens, norm_gain, *rest)
    layer_out, grad_logit, grad_out = pl.pallas_call(
        deliver_kernel,
        out_shape=(layer_shape, jax.ShapeDtypeStruct((4,), F32), grad_shape),
        in_specs=[vmem, smem, vmem],
        out_specs=(vmem, smem, vmem),
    )(*results)
    return layer_out.T, grad_logit, grad_out.T


def solution(mesh):
    return jax.shard_map(
        body,
        mesh=mesh,
        in_specs=(
            P("ctx", None),
            P(),
            P(None, "head"),
            P(None, "head"),
            P(None, "head"),
            P("head", None),
            P("head"),
            P("head"),
            P("ctx", None),
        ),
        out_specs=(P("ctx", "head"), P("head"), P("head", "ctx")),
        check_vma=False,
    )
```

```python
import math

import jax
import jax.numpy as jnp
from jax import lax
from jax.experimental import pallas as pl
from jax.experimental.pallas import tpu as pltpu
from jax.sharding import PartitionSpec as P

HEAD_SIZE = 128


EPSILON = 1e-06
BETA = 2.0 / 3.0
GAMMA = -0.1
ZETA = 1.1
PENALTY = 0.1
SCORE_POWER = 168.0 ** (-0.5) * math.log2(math.e)


MESH = pl.DeviceIdType.MESH
BF16 = jnp.bfloat16
F32 = jnp.float32
GRAD_ROWS = 336
OUT_ROWS = 672
HALF_OUT = 336
SPLIT = 176
INV_ROOT = 1.0 / math.sqrt(8192)


def hard_concrete(mask_logit, noise_draw):
    stretched = jax.nn.sigmoid(
        (jnp.log(noise_draw) - jnp.log(1.0 - noise_draw) + mask_logit) / BETA
    )
    shifted = stretched * (ZETA - GAMMA) + GAMMA
    gate_value = jnp.clip(shifted, 0.0, 1.0)
    inside = jnp.logical_and(shifted > 0.0, shifted < 1.0)
    gate_slope = jnp.where(inside, (ZETA - GAMMA) * stretched * (1.0 - stretched) / BETA, 0.0)
    expected = jax.nn.sigmoid(mask_logit - BETA * math.log(-GAMMA / ZETA))
    return (gate_value, gate_slope, PENALTY * expected * (1.0 - expected))


class Links:
    def __init__(self, send, recv):
        self.send, self.recv, self.count, self.open = send, recv, 0, []

    def start(self, source, target, device):
        copy = pltpu.make_async_remote_copy(
            src_ref=source,
            dst_ref=target,
            send_sem=self.send.at[self.count],
            recv_sem=self.recv.at[self.count],
            device_id=device,
            device_id_type=MESH,
        )
        self.count += 1
        copy.start()
        self.open.append(copy)
        return copy

    def finish(self):
        for copy in self.open:
            copy.wait_send()


def wide(value):
    return value.astype(F32)


def layer_kernel(
    tokens, gain, wq, wk, wv, wout, mask_logit, noise_draw, cot,
    layer_out, gate_out, grad_out,
    rows_in, cot_in, first_w, second_w, scale, keys_at, values_at, relay_k, relay_v, queries, top, low, acc, att, gated,
    grad, grad_in, line, line_in, out, out_core, out_in, gate_acc, gate_in, load, send, recv,
):
    ctx, head = lax.axis_index("ctx"), lax.axis_index("head")
    px, py = ctx // 4, ctx % 4
    pz, core = head // 2, head % 2

    def at_x(step):
        return ((px + step) % 4 * 4 + py, head)

    def at_y(step):
        return (px * 4 + (py + step) % 4, head)

    def at_z(step):
        return (ctx, (pz + step) % 4 * 2 + core)

    sibling = (ctx, pz * 2 + (1 - core))
    places = {"x": (px, at_x), "y": (py, at_y)}
    next_block = ((ctx + 1) % 16, head)
    two_on = ((px * 4 + (py + 1) % 4 + 2) % 16, head)
    back = (ctx + 14) % 16
    passer = (back // 4 * 4 + (back % 4 + 3) % 4, head)
    peers = [at(step) for at in (at_x, at_y) for step in (1, 2, 3)] + [at_z(1), at_z(3), sibling]
    peers += [((ctx + 15) % 16, head), passer]
    barrier = pltpu.get_barrier_semaphore()
    for peer in peers:
        pl.semaphore_signal(barrier, inc=1, device_id=peer, device_id_type=MESH)

    def fetch(number, source, target):
        copy = pltpu.make_async_copy(source, target, load.at[number])
        copy.start()
        return copy

    quarter = [pl.ds(128 * part, 128) for part in range(4)]
    token_loads = [fetch(part, tokens.at[rows], rows_in.at[rows]) for part, rows in enumerate(quarter)]
    weight_loads = []
    weight_copies = [
        (4, wk.at[:, pl.ds(0, 128)], first_w.at[:, pl.ds(0, 128)]),
        (5, wv.at[:, pl.ds(0, 128)], first_w.at[:, pl.ds(128, 128)]),
        (6, wk.at[:, pl.ds(128, 128)], first_w.at[:, pl.ds(256, 128)]),
        (7, wv.at[:, pl.ds(128, 128)], first_w.at[:, pl.ds(384, 128)]),
        (8, wq, second_w),
    ]

    strip = 768

    def cot_load(index):
        columns = pl.ds(pl.multiple_of(index * strip, 128), strip)
        return pltpu.make_async_copy(cot.at[:, columns], cot_in.at[:, columns], load.at[9 + index])

    def wout_load(index):
        columns = pl.ds(pl.multiple_of(index * strip, 128), strip)
        return pltpu.make_async_copy(wout.at[:, columns], rows_in.at[:, columns], load.at[16 + index])

    for part in range(4):
        token_loads[part].wait()
        for copy in weight_copies[0:2] if part == 0 else weight_copies[2:4] if part == 2 else weight_copies[4:] if part == 3 else []:
            weight_loads.append(fetch(*copy))

        def weigh(index, carry, part=part):
            rows = pl.ds(pl.multiple_of(part * 128 + index * 32, 32), 32)
            total = jnp.zeros((32, 128), F32)
            for tile in range(42):
                columns = slice(128 * tile, 128 * tile + 128)
                value = rows_in[rows, columns]
                total += wide(value) * wide(value)
                rows_in[rows, columns] = value * gain[columns][None, :]
            scale[rows, :] = total
            return carry

        lax.fori_loop(0, 4, weigh, 0)

    for index in range(7):
        cot_load(index).start()
    moment = jnp.sum(scale[...], axis=1, keepdims=True) * (1.0 / 5376)
    scale[...] = jnp.broadcast_to(lax.rsqrt(moment + EPSILON), (512, 128))

    def project(weight):
        product = jnp.dot(rows_in[...], weight, preferred_element_type=F32)
        return (product * jnp.concatenate([scale[...]] * (weight.shape[1] // 128), axis=1)).astype(BF16)

    links = Links(send, recv)

    def keys_and_values(pair):
        for copy in weight_loads[2 * pair : 2 * pair + 2]:
            copy.wait()
        both = project(first_w[:, 256 * pair : 256 * pair + 256])
        keys_at[0, pair] = both[:, 0:128]
        values_at[0, pair] = both[:, 128:256].T

    def pass_on(sources, targets, device):
        return [links.start(source, target, device) for source, target in zip(sources, targets)]

    def arrive(copies):
        for copy in copies:
            copy.wait_recv()

    def held(slot, pair):
        return keys_at.at[slot, pair], values_at.at[slot, pair]

    keys_and_values(0)
    pl.semaphore_wait(barrier, len(peers))
    hop0 = pass_on(held(0, 0), held(1, 0), next_block)
    keys_and_values(1)
    back1 = pass_on(held(0, 1), (relay_k, relay_v), at_y(3))
    weight_loads[4].wait()
    queries[...] = project(second_w[...])

    for index in range(7):
        wout_load(index).start()

    def attend(slot, pair):
        square = (128, 128)
        triangle = lax.broadcasted_iota(jnp.int32, square, 0) <= lax.broadcasted_iota(jnp.int32, square, 1)
        for block in range(4):
            rows = pl.ds(128 * block, 128)
            start, stop = (0, 128 * (block + 1)) if slot == 0 else (0, 512) if slot == 1 else (128 * block, 512)
            keys = keys_at[slot, pair, start:stop, :]
            values = values_at[slot, pair, :, start:stop]
            for number in (2 * pair, 2 * pair + 1):
                here, one = pl.ds(128 * number, 128), pl.ds(number, 1)
                scores = lax.dot_general(
                    keys, queries[rows, here], (((1,), (1,)), ((), ())), preferred_element_type=F32
                )
                if slot == 0:
                    last = jnp.where(triangle, scores[128 * block :], -jnp.inf)
                    scores = jnp.concatenate([scores[: 128 * block], last], axis=0) if block else last
                elif slot == 2:
                    edge = jnp.where(triangle, -jnp.inf, scores[:128])
                    scores = jnp.concatenate([edge, scores[128:]], axis=0) if block < 3 else edge
                peak = jnp.max(scores, axis=0, keepdims=True)
                if slot > 0:
                    before = top[one, rows]
                    peak = jnp.maximum(before, peak)
                    fade = jnp.exp2((before - peak) * SCORE_POWER)
                lifted = jnp.exp2((scores - peak) * SCORE_POWER)
                total = jnp.sum(lifted, axis=0, keepdims=True)
                mixed = jnp.dot(values, lifted.astype(BF16), preferred_element_type=F32)
                top[one, rows] = peak
                if slot > 0:
                    low[one, rows] = low[one, rows] * fade + total
                    acc[here, rows] = acc[here, rows] * fade + mixed
                else:
                    low[one, rows] = total
                    acc[here, rows] = mixed

    def close(pair):
        for number in (2 * pair, 2 * pair + 1):
            here = pl.ds(128 * number, 128)
            result = (acc[here, :] * (1.0 / low[pl.ds(number, 1), :])).astype(BF16)
            att[here, :] = result
            gated[here, :] = (wide(result) * gates[number][0:1, 0:1]).astype(BF16)

    attend(0, 0)
    arrive(hop0)
    far0 = pass_on(held(1, 0), held(2, 0), next_block)
    attend(0, 1)

    def turn_cot(index, carry):
        cot_load(index).wait()
        columns = pl.ds(pl.multiple_of(index * strip, 128), strip)
        second_w[columns, :] = cot_in[:, columns].T
        return carry

    lax.fori_loop(0, 7, turn_cot, 0)
    hop1 = pass_on(held(0, 1), held(1, 1), next_block)
    arrive(back1)
    far1 = pass_on((relay_k, relay_v), held(2, 1), two_on)

    @pl.when(ctx >= 1)
    def _():
        attend(1, 0)

    def turn_wout(index, carry):
        wout_load(index).wait()
        columns = pl.ds(pl.multiple_of(index * strip, 128), strip)
        first_w[columns, :] = rows_in[:, columns].T
        return carry

    lax.fori_loop(0, 7, turn_wout, 0)
    cot_t, wout_t = second_w, first_w

    def block_of(number, first, target, half):
        if first == "y":
            return grad.at[number, pl.ds(2 * half, 2), target]
        return grad.at[number, target, pl.ds(2 * half, 2)]

    firsts = ["y", "x", "y", "x"]
    gate_acc[...] = jnp.zeros_like(gate_acc)
    gate_in[0] = jnp.zeros((8, 128), F32)
    tall = 4 * GRAD_ROWS

    def grad_pair(pair):
        def chunk(index, carry):
            rows = pl.ds(pl.multiple_of(index * tall, 16), tall)
            product = lax.dot_general(
                cot_t[rows, :], att[256 * pair : 256 * pair + 256, :], (((1,), (1,)), ((), ())),
                preferred_element_type=F32,
            )
            for side in range(2):
                number = 2 * pair + side
                mine = product[:, 128 * side : 128 * side + 128]
                grad[number, index] = mine.astype(BF16).reshape(4, GRAD_ROWS, 128)
                weighed = mine * wide(wout_t[rows, 128 * number : 128 * number + 128])
                gate_acc[number] += jnp.sum(weighed.reshape(tall // 8, 8, 128), axis=0)
            return carry

        lax.fori_loop(0, 4, chunk, 0)

    stage1 = {}

    def send_first(number):
        first = firsts[number]
        place, at = places[first]
        far, after, before = (place + 2) % 4, (place + 1) % 4, (place + 3) % 4
        box = grad_in.at[number]
        stage1[number] = [
            links.start(block_of(number, first, far, 0), box.at[0], at(1)),
            links.start(block_of(number, first, far, 1), box.at[1], at(3)),
            links.start(block_of(number, first, before, 0), box.at[2], at(3)),
            links.start(block_of(number, first, after, 1), box.at[3], at(1)),
        ]

    def relay_first(number):
        first = firsts[number]
        place, at = places[first]
        after, before = (place + 1) % 4, (place + 3) % 4
        box = grad_in.at[number]
        for slot, target, half, step in ((0, after, 0, 1), (1, before, 1, 3)):
            stage1[number][slot].wait_recv()
            box[slot] = (wide(box[slot]) + wide(block_of(number, first, target, half)[...])).astype(BF16)
            stage1[number].append(links.start(box.at[slot], box.at[4 + slot], at(step)))

    def end_first(number):
        first = firsts[number]
        place, _ = places[first]
        box = grad_in.at[number]
        for half in range(2):
            stage1[number][2 + half].wait_recv()
            stage1[number][4 + half].wait_recv()
            total = wide(block_of(number, first, place, half)[...]) + wide(box[2 + half]) + wide(box[4 + half])
            line[number, pl.ds(2 * half, 2)] = total.astype(BF16)

    stage2 = {}
    cuts = (pl.ds(0, SPLIT), pl.ds(SPLIT, GRAD_ROWS - SPLIT))
    sizes = (pl.ds(0, SPLIT), pl.ds(0, GRAD_ROWS - SPLIT))

    def send_second(number):
        place, at = places["x" if firsts[number] == "y" else "y"]
        far, after, before = (place + 2) % 4, (place + 1) % 4, (place + 3) % 4
        mine, box = line.at[number], line_in.at[number]
        stage2[number] = [
            links.start(mine.at[far, cuts[0]], box.at[0, sizes[0]], at(1)),
            links.start(mine.at[far, cuts[1]], box.at[1, sizes[1]], at(3)),
            links.start(mine.at[before, cuts[0]], box.at[2, sizes[0]], at(3)),
            links.start(mine.at[after, cuts[1]], box.at[3, sizes[1]], at(1)),
        ]

    def relay_second(number):
        place, at = places["x" if firsts[number] == "y" else "y"]
        after, before = (place + 1) % 4, (place + 3) % 4
        mine, box = line.at[number], line_in.at[number]
        for slot, target, step in ((0, after, 1), (1, before, 3)):
            stage2[number][slot].wait_recv()
            part = box.at[slot, sizes[slot]]
            part[...] = (wide(part[...]) + wide(mine[target, cuts[slot]])).astype(BF16)
            stage2[number].append(links.start(part, box.at[4 + slot, sizes[slot]], at(step)))

    def end_second(number):
        place, _ = places["x" if firsts[number] == "y" else "y"]
        mine, box = line.at[number], line_in.at[number]
        for half in range(2):
            stage2[number][2 + half].wait_recv()
            stage2[number][4 + half].wait_recv()
            total = (
                wide(mine[place, cuts[half]])
                + wide(box[2 + half, sizes[half]])
                + wide(box[4 + half, sizes[half]])
            )
            grad_out[cuts[half], 128 * number : 128 * number + 128] = total * (gates[number][0:1, 0:1] * INV_ROOT)

    across = []

    def out_part(place):
        rows = pl.ds(pl.multiple_of(place * (2 * OUT_ROWS), 16), 2 * OUT_ROWS)
        product = jnp.dot(wout_t[rows, :], gated[...], preferred_element_type=F32).astype(BF16)
        out[place] = product.reshape(2, OUT_ROWS, 512)
        across.append(links.start(out.at[place, 1 - core], out_core.at[place], sibling))

    gates, slopes, penalties = zip(
        *(
            hard_concrete(jnp.full((8, 128), mask_logit[number], F32), jnp.full((8, 128), noise_draw[number], F32))
            for number in range(4)
        )
    )
    arrive(far0)

    @pl.when(ctx >= 2)
    def _():
        attend(2, 0)

    close(0)
    grad_pair(0)
    send_first(0)
    send_first(1)
    arrive(hop1)

    @pl.when(ctx >= 1)
    def _():
        attend(1, 1)

    arrive(far1)

    @pl.when(ctx >= 2)
    def _():
        attend(2, 1)

    close(1)
    order = [(pz + step) % 4 for step in (2, 1, 3, 0)]
    for place in order[:3]:
        out_part(place)

    def add_core(index):
        across[index].wait_recv()
        place = order[index]

        def piece(step, carry):
            rows = pl.ds(pl.multiple_of(step * 112, 16), 112)
            out_core[place, rows] = (wide(out[place, core, rows]) + wide(out_core[place, rows])).astype(BF16)
            return carry

        lax.fori_loop(0, OUT_ROWS // 112, piece, 0)

    far, after, before = order[0], order[1], order[2]
    upper, lower = pl.ds(0, HALF_OUT), pl.ds(HALF_OUT, HALF_OUT)
    add_core(0)
    ring = [
        links.start(out_core.at[far, upper], out_in.at[0], at_z(1)),
        links.start(out_core.at[far, lower], out_in.at[1], at_z(3)),
    ]
    relay_first(0)
    relay_first(1)
    grad_pair(1)
    send_first(2)
    send_first(3)
    add_core(1)
    add_core(2)
    ring += [
        links.start(out_core.at[before, upper], out_in.at[2], at_z(3)),
        links.start(out_core.at[after, lower], out_in.at[3], at_z(1)),
    ]

    out_part(order[3])

    for number in range(4):
        gate_in[0, pl.ds(number, 1)] = jnp.sum(gate_acc[number], axis=0, keepdims=True)
    gate_y = [links.start(gate_in.at[0], gate_in.at[step], at_y(step)) for step in (1, 2, 3)]
    add_core(3)
    for number in (0, 1):
        end_first(number)
        send_second(number)
    relay_first(2)
    relay_first(3)
    for slot, target, rows, step in ((0, after, 0, 1), (1, before, HALF_OUT, 3)):
        ring[slot].wait_recv()

        def piece(index, carry, slot=slot, target=target, rows=rows):
            here = pl.ds(pl.multiple_of(index * 112, 16), 112)
            there = pl.ds(pl.multiple_of(index * 112 + rows, 16), 112)
            out_in[slot, here] = (wide(out_in[slot, here]) + wide(out_core[target, there])).astype(BF16)
            return carry

        lax.fori_loop(0, HALF_OUT // 112, piece, 0)
        ring.append(links.start(out_in.at[slot], out_in.at[4 + slot], at_z(step)))

    for copy in gate_y:
        copy.wait_recv()
    gate_in[4] = gate_in[0] + gate_in[1] + gate_in[2] + gate_in[3]
    gate_x = [links.start(gate_in.at[4], gate_in.at[4 + step], at_x(step)) for step in (1, 2, 3)]
    relay_second(0)
    relay_second(1)
    for number in (2, 3):
        end_first(number)
        send_second(number)
    end_second(0)
    end_second(1)
    for copy in gate_x:
        copy.wait_recv()
    gate_sum = gate_in[4] + gate_in[5] + gate_in[6] + gate_in[7]
    for number in range(4):
        product = jnp.sum(gate_sum[number : number + 1, :], axis=1, keepdims=True)
        answer = product * INV_ROOT * slopes[number] + penalties[number]
        gate_out[pl.ds(number, 1), :] = jnp.broadcast_to(answer[0:1, :], (1, 128))
    relay_second(2)
    relay_second(3)
    for half in range(2):
        ring[2 + half].wait_recv()
        ring[4 + half].wait_recv()

        def piece(index, carry, half=half):
            here = pl.ds(pl.multiple_of(index * 112, 16), 112)
            there = pl.ds(pl.multiple_of(index * 112 + half * HALF_OUT, 16), 112)
            total = wide(out_core[pz, there]) + wide(out_in[2 + half, here]) + wide(out_in[4 + half, here])
            layer_out[there, :] = total.astype(BF16)
            return carry

        lax.fori_loop(0, HALF_OUT // 112, piece, 0)
    end_second(2)
    end_second(3)
    links.finish()


def deliver_kernel(layer_in, gate_in, grad_in, layer_out, gate_out, grad_out):
    layer_out[...] = layer_in[...]
    grad_out[...] = grad_in[...]
    for number in range(4):
        gate_out[number] = gate_in[number, 0]


def body(*args):
    vmem = pl.BlockSpec(memory_space=pltpu.VMEM)
    smem = pl.BlockSpec(memory_space=pltpu.SMEM)
    hbm = pl.BlockSpec(memory_space=pl.ANY)
    wide_w = pltpu.VMEM((5376, 512), BF16)
    tokens, norm_gain, *rest = args
    layer_shape = jax.ShapeDtypeStruct((OUT_ROWS, 512), BF16)
    grad_shape = jax.ShapeDtypeStruct((GRAD_ROWS, 512), F32)
    results = pl.pallas_call(
        layer_kernel,
        out_shape=(layer_shape, jax.ShapeDtypeStruct((8, 128), F32), grad_shape),
        in_specs=[hbm, vmem, hbm, hbm, hbm, hbm, smem, smem, hbm],
        out_specs=(vmem,) * 3,
        scratch_shapes=[
            pltpu.VMEM((512, 5376), BF16),
            pltpu.VMEM((512, 5376), BF16),
            wide_w,
            wide_w,
            pltpu.VMEM((512, 128), F32),
            pltpu.VMEM((3, 2, 512, 128), BF16),
            pltpu.VMEM((3, 2, 128, 512), BF16),
            pltpu.VMEM((512, 128), BF16),
            pltpu.VMEM((128, 512), BF16),
            pltpu.VMEM((512, 512), BF16),
            pltpu.VMEM((8, 512), F32),
            pltpu.VMEM((8, 512), F32),
            pltpu.VMEM((512, 512), F32),
            pltpu.VMEM((512, 512), BF16),
            pltpu.VMEM((512, 512), BF16),
            pltpu.VMEM((4, 4, 4, GRAD_ROWS, 128), BF16),
            pltpu.VMEM((4, 6, 2, GRAD_ROWS, 128), BF16),
            pltpu.VMEM((4, 4, GRAD_ROWS, 128), BF16),
            pltpu.VMEM((4, 6, SPLIT, 128), BF16),
            pltpu.VMEM((4, 2, OUT_ROWS, 512), BF16),
            pltpu.VMEM((4, OUT_ROWS, 512), BF16),
            pltpu.VMEM((6, HALF_OUT, 512), BF16),
            pltpu.VMEM((4, 8, 128), F32),
            pltpu.VMEM((8, 8, 128), F32),
            pltpu.SemaphoreType.DMA((23,)),
            pltpu.SemaphoreType.DMA((74,)),
            pltpu.SemaphoreType.DMA((74,)),
        ],
        compiler_params=pltpu.CompilerParams(
            collective_id=0, has_side_effects=True, vmem_limit_bytes=58 * 2**20
        ),
    )(tokens, norm_gain, *rest)
    layer_out, grad_logit, grad_out = pl.pallas_call(
        deliver_kernel,
        out_shape=(layer_shape, jax.ShapeDtypeStruct((4,), F32), grad_shape),
        in_specs=[vmem, smem, vmem],
        out_specs=(vmem, smem, vmem),
    )(*results)
    return layer_out.T, grad_logit, grad_out.T


def solution(mesh):
    return jax.shard_map(
        body,
        mesh=mesh,
        in_specs=(
            P("ctx", None),
            P(),
            P(None, "head"),
            P(None, "head"),
            P(None, "head"),
            P("head", None),
            P("head"),
            P("head"),
            P("ctx", None),
        ),
        out_specs=(P("ctx", "head"), P("head"), P("head", "ctx")),
        check_vma=False,
    )
```

```python
import math

import jax
import jax.numpy as jnp
from jax import lax
from jax.experimental import pallas as pl
from jax.experimental.pallas import tpu as pltpu
from jax.sharding import PartitionSpec as P

HEAD_SIZE = 128


EPSILON = 1e-06
BETA = 2.0 / 3.0
GAMMA = -0.1
ZETA = 1.1
PENALTY = 0.1
SCORE_POWER = 168.0 ** (-0.5) * math.log2(math.e)


MESH = pl.DeviceIdType.MESH
BF16 = jnp.bfloat16
F32 = jnp.float32
GRAD_ROWS = 336
OUT_ROWS = 672
HALF_OUT = 336
SPLIT = 176
INV_ROOT = 1.0 / math.sqrt(8192)


def hard_concrete(mask_logit, noise_draw):
    stretched = jax.nn.sigmoid(
        (jnp.log(noise_draw) - jnp.log(1.0 - noise_draw) + mask_logit) / BETA
    )
    shifted = stretched * (ZETA - GAMMA) + GAMMA
    gate_value = jnp.clip(shifted, 0.0, 1.0)
    inside = jnp.logical_and(shifted > 0.0, shifted < 1.0)
    gate_slope = jnp.where(inside, (ZETA - GAMMA) * stretched * (1.0 - stretched) / BETA, 0.0)
    expected = jax.nn.sigmoid(mask_logit - BETA * math.log(-GAMMA / ZETA))
    return (gate_value, gate_slope, PENALTY * expected * (1.0 - expected))


class Links:
    def __init__(self, send, recv):
        self.send, self.recv, self.count, self.open = send, recv, 0, []

    def start(self, source, target, device):
        copy = pltpu.make_async_remote_copy(
            src_ref=source,
            dst_ref=target,
            send_sem=self.send.at[self.count],
            recv_sem=self.recv.at[self.count],
            device_id=device,
            device_id_type=MESH,
        )
        self.count += 1
        copy.start()
        self.open.append(copy)
        return copy

    def finish(self):
        for copy in self.open:
            copy.wait_send()


def wide(value):
    return value.astype(F32)


def layer_kernel(
    tokens, gain, wq, wk, wv, wout, mask_logit, noise_draw, cot,
    layer_out, gate_out, grad_out,
    rows_in, cot_in, first_w, second_w, scale, keys_at, values_at, relay_k, relay_v, queries, top, low, acc, att, gated,
    grad, grad_in, line, line_in, out, out_core, out_in, gate_acc, gate_in, load, send, recv,
):
    ctx, head = lax.axis_index("ctx"), lax.axis_index("head")
    px, py = ctx // 4, ctx % 4
    pz, core = head // 2, head % 2

    def at_x(step):
        return ((px + step) % 4 * 4 + py, head)

    def at_y(step):
        return (px * 4 + (py + step) % 4, head)

    def at_z(step):
        return (ctx, (pz + step) % 4 * 2 + core)

    sibling = (ctx, pz * 2 + (1 - core))
    places = {"x": (px, at_x), "y": (py, at_y)}
    next_block = ((ctx + 1) % 16, head)
    two_on = ((px * 4 + (py + 1) % 4 + 2) % 16, head)
    back = (ctx + 14) % 16
    passer = (back // 4 * 4 + (back % 4 + 3) % 4, head)
    peers = [at(step) for at in (at_x, at_y) for step in (1, 2, 3)] + [at_z(1), at_z(3), sibling]
    peers += [((ctx + 15) % 16, head), passer]
    barrier = pltpu.get_barrier_semaphore()
    for peer in peers:
        pl.semaphore_signal(barrier, inc=1, device_id=peer, device_id_type=MESH)

    def fetch(number, source, target):
        copy = pltpu.make_async_copy(source, target, load.at[number])
        copy.start()
        return copy

    quarter = [pl.ds(128 * part, 128) for part in range(4)]
    token_loads = [fetch(part, tokens.at[rows], rows_in.at[rows]) for part, rows in enumerate(quarter)]
    weight_loads = []
    weight_copies = [
        (4, wk.at[:, pl.ds(0, 128)], first_w.at[:, pl.ds(0, 128)]),
        (5, wv.at[:, pl.ds(0, 128)], first_w.at[:, pl.ds(128, 128)]),
        (6, wk.at[:, pl.ds(128, 128)], first_w.at[:, pl.ds(256, 128)]),
        (7, wv.at[:, pl.ds(128, 128)], first_w.at[:, pl.ds(384, 128)]),
        (8, wq, second_w),
    ]

    strip = 768

    def cot_load(index):
        columns = pl.ds(pl.multiple_of(index * strip, 128), strip)
        return pltpu.make_async_copy(cot.at[:, columns], cot_in.at[:, columns], load.at[9 + index])

    def wout_load(index):
        columns = pl.ds(pl.multiple_of(index * strip, 128), strip)
        return pltpu.make_async_copy(wout.at[:, columns], rows_in.at[:, columns], load.at[16 + index])

    for part in range(4):
        token_loads[part].wait()
        for copy in weight_copies[0:2] if part == 0 else weight_copies[2:4] if part == 2 else weight_copies[4:] if part == 3 else []:
            weight_loads.append(fetch(*copy))

        def weigh(index, carry, part=part):
            rows = pl.ds(pl.multiple_of(part * 128 + index * 32, 32), 32)
            total = jnp.zeros((32, 128), F32)
            for tile in range(42):
                columns = slice(128 * tile, 128 * tile + 128)
                value = rows_in[rows, columns]
                total += wide(value) * wide(value)
                rows_in[rows, columns] = value * gain[columns][None, :]
            scale[rows, :] = total
            return carry

        lax.fori_loop(0, 4, weigh, 0)

    for index in range(7):
        cot_load(index).start()
    moment = jnp.sum(scale[...], axis=1, keepdims=True) * (1.0 / 5376)
    scale[...] = jnp.broadcast_to(lax.rsqrt(moment + EPSILON), (512, 128))

    def project(weight):
        product = jnp.dot(rows_in[...], weight, preferred_element_type=F32)
        return (product * jnp.concatenate([scale[...]] * (weight.shape[1] // 128), axis=1)).astype(BF16)

    links = Links(send, recv)

    def keys_and_values(pair):
        for copy in weight_loads[2 * pair : 2 * pair + 2]:
            copy.wait()
        both = project(first_w[:, 256 * pair : 256 * pair + 256])
        keys_at[0, pair] = both[:, 0:128]
        values_at[0, pair] = both[:, 128:256].T

    def pass_on(sources, targets, device):
        return [links.start(source, target, device) for source, target in zip(sources, targets)]

    def arrive(copies):
        for copy in copies:
            copy.wait_recv()

    def held(slot, pair):
        return keys_at.at[slot, pair], values_at.at[slot, pair]

    keys_and_values(0)
    pl.semaphore_wait(barrier, len(peers))
    hop0 = pass_on(held(0, 0), held(1, 0), next_block)
    keys_and_values(1)
    back1 = pass_on(held(0, 1), (relay_k, relay_v), at_y(3))
    weight_loads[4].wait()
    queries[...] = project(second_w[...])

    for index in range(7):
        wout_load(index).start()

    def attend(slot, pair):
        square = (128, 128)
        triangle = lax.broadcasted_iota(jnp.int32, square, 0) <= lax.broadcasted_iota(jnp.int32, square, 1)
        for block in range(4):
            rows = pl.ds(128 * block, 128)
            start, stop = (0, 128 * (block + 1)) if slot == 0 else (0, 512) if slot == 1 else (128 * block, 512)
            keys = keys_at[slot, pair, start:stop, :]
            values = values_at[slot, pair, :, start:stop]
            for number in (2 * pair, 2 * pair + 1):
                here, one = pl.ds(128 * number, 128), pl.ds(number, 1)
                scores = lax.dot_general(
                    keys, queries[rows, here], (((1,), (1,)), ((), ())), preferred_element_type=F32
                )
                if slot == 0:
                    last = jnp.where(triangle, scores[128 * block :], -jnp.inf)
                    scores = jnp.concatenate([scores[: 128 * block], last], axis=0) if block else last
                elif slot == 2:
                    edge = jnp.where(triangle, -jnp.inf, scores[:128])
                    scores = jnp.concatenate([edge, scores[128:]], axis=0) if block < 3 else edge
                peak = jnp.max(scores, axis=0, keepdims=True)
                if slot > 0:
                    before = top[one, rows]
                    peak = jnp.maximum(before, peak)
                    fade = jnp.exp2((before - peak) * SCORE_POWER)
                lifted = jnp.exp2((scores - peak) * SCORE_POWER)
                total = jnp.sum(lifted, axis=0, keepdims=True)
                mixed = jnp.dot(values, lifted.astype(BF16), preferred_element_type=F32)
                top[one, rows] = peak
                if slot > 0:
                    low[one, rows] = low[one, rows] * fade + total
                    acc[here, rows] = acc[here, rows] * fade + mixed
                else:
                    low[one, rows] = total
                    acc[here, rows] = mixed

    def close(pair):
        for number in (2 * pair, 2 * pair + 1):
            here = pl.ds(128 * number, 128)
            result = (acc[here, :] * (1.0 / low[pl.ds(number, 1), :])).astype(BF16)
            att[here, :] = result
            gated[here, :] = (wide(result) * gates[number][0:1, 0:1]).astype(BF16)

    attend(0, 0)
    arrive(hop0)
    far0 = pass_on(held(1, 0), held(2, 0), next_block)
    attend(0, 1)

    def turn_cot(index, carry):
        cot_load(index).wait()
        columns = pl.ds(pl.multiple_of(index * strip, 128), strip)
        second_w[columns, :] = cot_in[:, columns].T
        return carry

    lax.fori_loop(0, 7, turn_cot, 0)
    hop1 = pass_on(held(0, 1), held(1, 1), next_block)
    arrive(back1)
    far1 = pass_on((relay_k, relay_v), held(2, 1), two_on)

    @pl.when(ctx >= 1)
    def _():
        attend(1, 0)

    def turn_wout(index, carry):
        wout_load(index).wait()
        columns = pl.ds(pl.multiple_of(index * strip, 128), strip)
        first_w[columns, :] = rows_in[:, columns].T
        return carry

    lax.fori_loop(0, 7, turn_wout, 0)
    cot_t, wout_t = second_w, first_w

    def block_of(number, first, target, half):
        if first == "y":
            return grad.at[number, pl.ds(2 * half, 2), target]
        return grad.at[number, target, pl.ds(2 * half, 2)]

    firsts = ["y", "x", "y", "x"]
    gate_acc[...] = jnp.zeros_like(gate_acc)
    gate_in[0] = jnp.zeros((8, 128), F32)
    tall = 4 * GRAD_ROWS

    def grad_pair(pair):
        def chunk(index, carry):
            rows = pl.ds(pl.multiple_of(index * tall, 16), tall)
            product = lax.dot_general(
                cot_t[rows, :], att[256 * pair : 256 * pair + 256, :], (((1,), (1,)), ((), ())),
                preferred_element_type=F32,
            )
            for side in range(2):
                number = 2 * pair + side
                mine = product[:, 128 * side : 128 * side + 128]
                grad[number, index] = mine.astype(BF16).reshape(4, GRAD_ROWS, 128)
                weighed = mine * wide(wout_t[rows, 128 * number : 128 * number + 128])
                gate_acc[number] += jnp.sum(weighed.reshape(tall // 8, 8, 128), axis=0)
            return carry

        lax.fori_loop(0, 4, chunk, 0)

    stage1 = {}

    def send_first(number):
        first = firsts[number]
        place, at = places[first]
        far, after, before = (place + 2) % 4, (place + 1) % 4, (place + 3) % 4
        box = grad_in.at[number]
        stage1[number] = [
            links.start(block_of(number, first, far, 0), box.at[0], at(1)),
            links.start(block_of(number, first, far, 1), box.at[1], at(3)),
            links.start(block_of(number, first, before, 0), box.at[2], at(3)),
            links.start(block_of(number, first, after, 1), box.at[3], at(1)),
        ]

    def relay_first(number):
        first = firsts[number]
        place, at = places[first]
        after, before = (place + 1) % 4, (place + 3) % 4
        box = grad_in.at[number]
        for slot, target, half, step in ((0, after, 0, 1), (1, before, 1, 3)):
            stage1[number][slot].wait_recv()
            box[slot] = (wide(box[slot]) + wide(block_of(number, first, target, half)[...])).astype(BF16)
            stage1[number].append(links.start(box.at[slot], box.at[4 + slot], at(step)))

    def end_first(number):
        first = firsts[number]
        place, _ = places[first]
        box = grad_in.at[number]
        for half in range(2):
            stage1[number][2 + half].wait_recv()
            stage1[number][4 + half].wait_recv()
            total = wide(block_of(number, first, place, half)[...]) + wide(box[2 + half]) + wide(box[4 + half])
            line[number, pl.ds(2 * half, 2)] = total.astype(BF16)

    stage2 = {}
    cuts = (pl.ds(0, SPLIT), pl.ds(SPLIT, GRAD_ROWS - SPLIT))
    sizes = (pl.ds(0, SPLIT), pl.ds(0, GRAD_ROWS - SPLIT))

    def send_second(number):
        place, at = places["x" if firsts[number] == "y" else "y"]
        far, after, before = (place + 2) % 4, (place + 1) % 4, (place + 3) % 4
        mine, box = line.at[number], line_in.at[number]
        stage2[number] = [
            links.start(mine.at[far, cuts[0]], box.at[0, sizes[0]], at(1)),
            links.start(mine.at[far, cuts[1]], box.at[1, sizes[1]], at(3)),
            links.start(mine.at[before, cuts[0]], box.at[2, sizes[0]], at(3)),
            links.start(mine.at[after, cuts[1]], box.at[3, sizes[1]], at(1)),
        ]

    def relay_second(number):
        place, at = places["x" if firsts[number] == "y" else "y"]
        after, before = (place + 1) % 4, (place + 3) % 4
        mine, box = line.at[number], line_in.at[number]
        for slot, target, step in ((0, after, 1), (1, before, 3)):
            stage2[number][slot].wait_recv()
            part = box.at[slot, sizes[slot]]
            part[...] = (wide(part[...]) + wide(mine[target, cuts[slot]])).astype(BF16)
            stage2[number].append(links.start(part, box.at[4 + slot, sizes[slot]], at(step)))

    def end_second(number):
        place, _ = places["x" if firsts[number] == "y" else "y"]
        mine, box = line.at[number], line_in.at[number]
        for half in range(2):
            stage2[number][2 + half].wait_recv()
            stage2[number][4 + half].wait_recv()
            total = (
                wide(mine[place, cuts[half]])
                + wide(box[2 + half, sizes[half]])
                + wide(box[4 + half, sizes[half]])
            )
            grad_out[cuts[half], 128 * number : 128 * number + 128] = total * (gates[number][0:1, 0:1] * INV_ROOT)

    across = []

    def out_part(place):
        rows = pl.ds(pl.multiple_of(place * (2 * OUT_ROWS), 16), 2 * OUT_ROWS)
        product = jnp.dot(wout_t[rows, :], gated[...], preferred_element_type=F32).astype(BF16)
        out[place] = product.reshape(2, OUT_ROWS, 512)
        across.append(links.start(out.at[place, 1 - core], out_core.at[place], sibling))

    gates, slopes, penalties = zip(
        *(
            hard_concrete(jnp.full((8, 128), mask_logit[number], F32), jnp.full((8, 128), noise_draw[number], F32))
            for number in range(4)
        )
    )
    arrive(far0)

    @pl.when(ctx >= 2)
    def _():
        attend(2, 0)

    close(0)
    grad_pair(0)
    send_first(0)
    send_first(1)
    arrive(hop1)

    @pl.when(ctx >= 1)
    def _():
        attend(1, 1)

    arrive(far1)

    @pl.when(ctx >= 2)
    def _():
        attend(2, 1)

    close(1)
    order = [(pz + step) % 4 for step in (2, 1, 3, 0)]
    for place in order[:3]:
        out_part(place)

    def add_core(index):
        across[index].wait_recv()
        place = order[index]

        def piece(step, carry):
            rows = pl.ds(pl.multiple_of(step * 112, 16), 112)
            out_core[place, rows] = (wide(out[place, core, rows]) + wide(out_core[place, rows])).astype(BF16)
            return carry

        lax.fori_loop(0, OUT_ROWS // 112, piece, 0)

    far, after, before = order[0], order[1], order[2]
    upper, lower = pl.ds(0, HALF_OUT), pl.ds(HALF_OUT, HALF_OUT)
    relay_first(0)
    relay_first(1)
    add_core(0)
    ring = [
        links.start(out_core.at[far, upper], out_in.at[0], at_z(1)),
        links.start(out_core.at[far, lower], out_in.at[1], at_z(3)),
    ]
    grad_pair(1)
    send_first(2)
    send_first(3)
    add_core(1)
    add_core(2)
    ring += [
        links.start(out_core.at[before, upper], out_in.at[2], at_z(3)),
        links.start(out_core.at[after, lower], out_in.at[3], at_z(1)),
    ]

    out_part(order[3])

    for number in range(4):
        gate_in[0, pl.ds(number, 1)] = jnp.sum(gate_acc[number], axis=0, keepdims=True)
    gate_y = [links.start(gate_in.at[0], gate_in.at[step], at_y(step)) for step in (1, 2, 3)]
    add_core(3)
    for number in (0, 1):
        end_first(number)
        send_second(number)
    relay_first(2)
    relay_first(3)
    for slot, target, rows, step in ((0, after, 0, 1), (1, before, HALF_OUT, 3)):
        ring[slot].wait_recv()

        def piece(index, carry, slot=slot, target=target, rows=rows):
            here = pl.ds(pl.multiple_of(index * 112, 16), 112)
            there = pl.ds(pl.multiple_of(index * 112 + rows, 16), 112)
            out_in[slot, here] = (wide(out_in[slot, here]) + wide(out_core[target, there])).astype(BF16)
            return carry

        lax.fori_loop(0, HALF_OUT // 112, piece, 0)
        ring.append(links.start(out_in.at[slot], out_in.at[4 + slot], at_z(step)))

    for copy in gate_y:
        copy.wait_recv()
    gate_in[4] = gate_in[0] + gate_in[1] + gate_in[2] + gate_in[3]
    gate_x = [links.start(gate_in.at[4], gate_in.at[4 + step], at_x(step)) for step in (1, 2, 3)]
    relay_second(0)
    relay_second(1)
    for number in (2, 3):
        end_first(number)
        send_second(number)
    end_second(0)
    end_second(1)
    for copy in gate_x:
        copy.wait_recv()
    gate_sum = gate_in[4] + gate_in[5] + gate_in[6] + gate_in[7]
    for number in range(4):
        product = jnp.sum(gate_sum[number : number + 1, :], axis=1, keepdims=True)
        answer = product * INV_ROOT * slopes[number] + penalties[number]
        gate_out[pl.ds(number, 1), :] = jnp.broadcast_to(answer[0:1, :], (1, 128))
    relay_second(2)
    relay_second(3)
    for half in range(2):
        ring[2 + half].wait_recv()
        ring[4 + half].wait_recv()

        def piece(index, carry, half=half):
            here = pl.ds(pl.multiple_of(index * 112, 16), 112)
            there = pl.ds(pl.multiple_of(index * 112 + half * HALF_OUT, 16), 112)
            total = wide(out_core[pz, there]) + wide(out_in[2 + half, here]) + wide(out_in[4 + half, here])
            layer_out[there, :] = total.astype(BF16)
            return carry

        lax.fori_loop(0, HALF_OUT // 112, piece, 0)
    end_second(2)
    end_second(3)
    links.finish()


def deliver_kernel(layer_in, gate_in, grad_in, layer_out, gate_out, grad_out):
    layer_out[...] = layer_in[...]
    grad_out[...] = grad_in[...]
    for number in range(4):
        gate_out[number] = gate_in[number, 0]


def body(*args):
    vmem = pl.BlockSpec(memory_space=pltpu.VMEM)
    smem = pl.BlockSpec(memory_space=pltpu.SMEM)
    hbm = pl.BlockSpec(memory_space=pl.ANY)
    wide_w = pltpu.VMEM((5376, 512), BF16)
    tokens, norm_gain, *rest = args
    layer_shape = jax.ShapeDtypeStruct((OUT_ROWS, 512), BF16)
    grad_shape = jax.ShapeDtypeStruct((GRAD_ROWS, 512), F32)
    results = pl.pallas_call(
        layer_kernel,
        out_shape=(layer_shape, jax.ShapeDtypeStruct((8, 128), F32), grad_shape),
        in_specs=[hbm, vmem, hbm, hbm, hbm, hbm, smem, smem, hbm],
        out_specs=(vmem,) * 3,
        scratch_shapes=[
            pltpu.VMEM((512, 5376), BF16),
            pltpu.VMEM((512, 5376), BF16),
            wide_w,
            wide_w,
            pltpu.VMEM((512, 128), F32),
            pltpu.VMEM((3, 2, 512, 128), BF16),
            pltpu.VMEM((3, 2, 128, 512), BF16),
            pltpu.VMEM((512, 128), BF16),
            pltpu.VMEM((128, 512), BF16),
            pltpu.VMEM((512, 512), BF16),
            pltpu.VMEM((8, 512), F32),
            pltpu.VMEM((8, 512), F32),
            pltpu.VMEM((512, 512), F32),
            pltpu.VMEM((512, 512), BF16),
            pltpu.VMEM((512, 512), BF16),
            pltpu.VMEM((4, 4, 4, GRAD_ROWS, 128), BF16),
            pltpu.VMEM((4, 6, 2, GRAD_ROWS, 128), BF16),
            pltpu.VMEM((4, 4, GRAD_ROWS, 128), BF16),
            pltpu.VMEM((4, 6, SPLIT, 128), BF16),
            pltpu.VMEM((4, 2, OUT_ROWS, 512), BF16),
            pltpu.VMEM((4, OUT_ROWS, 512), BF16),
            pltpu.VMEM((6, HALF_OUT, 512), BF16),
            pltpu.VMEM((4, 8, 128), F32),
            pltpu.VMEM((8, 8, 128), F32),
            pltpu.SemaphoreType.DMA((23,)),
            pltpu.SemaphoreType.DMA((74,)),
            pltpu.SemaphoreType.DMA((74,)),
        ],
        compiler_params=pltpu.CompilerParams(
            collective_id=0, has_side_effects=True, vmem_limit_bytes=58 * 2**20
        ),
    )(tokens, norm_gain, *rest)
    layer_out, grad_logit, grad_out = pl.pallas_call(
        deliver_kernel,
        out_shape=(layer_shape, jax.ShapeDtypeStruct((4,), F32), grad_shape),
        in_specs=[vmem, smem, vmem],
        out_specs=(vmem, smem, vmem),
    )(*results)
    return layer_out.T, grad_logit, grad_out.T


def solution(mesh):
    return jax.shard_map(
        body,
        mesh=mesh,
        in_specs=(
            P("ctx", None),
            P(),
            P(None, "head"),
            P(None, "head"),
            P(None, "head"),
            P("head", None),
            P("head"),
            P("head"),
            P("ctx", None),
        ),
        out_specs=(P("ctx", "head"), P("head"), P("head", "ctx")),
        check_vma=False,
    )
```
